32 devices in a mesh: seq: 16 (over z, y, x), mdl: 2 (over core).
Axes of the slice: x: 2, y: 2, z: 4, core: 2. Of those that a mesh axis runs over, the one named last changes fastest.
Arguments:
- hidden_in: bfloat16 [32, 4, 2048], P(None, None, 'seq'), may hold values from -25 to 25
- cache_keys: bfloat16 [32, 512, 2048], P(None, 'seq', 'mdl'), may hold values from -250 to 250, as said below
- cache_values: bfloat16 [32, 512, 2048], P(None, 'seq', 'mdl'), may hold values from -6 to 6
- lengths: int32 [32], replicated, may hold values from 1 to 508, as said below
- query_weight: bfloat16 [2048, 2048], P('seq', 'mdl'), may hold values from -0.125 to 0.125
- key_weight: bfloat16 [2048, 2048], P('seq', 'mdl'), may hold values from -0.125 to 0.125
- value_weight: bfloat16 [2048, 2048], P('seq', 'mdl'), may hold values from -0.125 to 0.125
- out_weight: bfloat16 [2048, 2048], P('mdl', 'seq'), may hold values from -0.125 to 0.125
- gate_weight: bfloat16 [2048, 8192], P('seq', 'mdl'), may hold values from -0.125 to 0.125
- up_weight: bfloat16 [2048, 8192], P('seq', 'mdl'), may hold values from -0.125 to 0.125
- down_weight: bfloat16 [8192, 2048], P('mdl', 'seq'), may hold values from -0.0625 to 0.0625
Outputs:
- hidden_out: bfloat16 [32, 4, 2048], P(None, None, 'seq')
- new_cache_keys: bfloat16 [32, 512, 2048], P(None, 'seq', 'mdl')
- new_cache_values: bfloat16 [32, 512, 2048], P(None, 'seq', 'mdl')
The draws below stay inside these ranges and needn't reach their ends.
Inputs may be any that keep to these rules, and one draw needn't show every extreme that they name: `cache_keys`: keys are stored after their rotary embedding. `lengths`: at least one request has exactly 508 cached positions.
All inputs are finite; a program needn't handle non-finite values.
Results may differ from the reference program's by a relative error of at most 0.012.
The reference program's roundings to bfloat16 on the way (of `normed`, `attended`, `normed2` and `act`) count: a program that leaves them out, or rounds other values in their place, can miss the bound.
Values may be sent and summed in bfloat16 or wider, within the bound.
A program may use at most 64 MiB of HBM per device.

```python
import jax
import jax.numpy as jnp
from jax import lax

D = 2048
HEADS = 16
FF = 8192
HEAD_DIM = 128
REQ = 32
NEW = 4
MAXLEN = 512


def draw_hidden_in(key, part):
    parts_keys = jax.random.split(key, 2)
    column = jnp.arange(D, dtype=jnp.float32) / D
    row_scale = jnp.exp(jax.random.uniform(parts_keys[0], (REQ, NEW, 1), jnp.float32, jnp.log(0.2), jnp.log(2.0)))
    column_scale = 0.5 * jnp.exp(jnp.log(3.0) * column)
    entries = jnp.clip(jax.random.normal(parts_keys[1], (REQ, NEW, D), jnp.float32), -6.0, 6.0)
    return (row_scale * column_scale * entries).astype(jnp.bfloat16)


def draw_cache_keys(key, part):
    parts_keys = jax.random.split(key, 1)
    entries = jnp.clip(jax.random.normal(parts_keys[0], (REQ, MAXLEN, D), jnp.float32), -6.0, 6.0)
    return (3.0 * entries).astype(jnp.bfloat16)


def draw_lengths(key, part):
    parts_keys = jax.random.split(key, 4)
    longest = MAXLEN - NEW
    first_draw = jax.random.randint(parts_keys[0], (REQ,), 0, longest)
    second_draw = jax.random.randint(parts_keys[1], (REQ,), 0, longest)
    shifts = jax.random.randint(parts_keys[2], (REQ,), 0, 3)
    drawn = 1 + jnp.right_shift(first_draw * second_draw // longest, shifts)
    chosen = jax.random.randint(parts_keys[3], (), 0, REQ)
    return jnp.where(jnp.arange(REQ) == chosen, longest, drawn).astype(jnp.int32)


def steps_of(key, shape, cuts, smallest, largest):
    def one(position, blocks):
        draws = jax.random.uniform(jax.random.fold_in(jax.random.fold_in(key, 6), position), (blocks,), jnp.float32, smallest / len(cuts), largest / len(cuts))
        return jnp.repeat(jnp.exp(draws), shape[position] // blocks).reshape((-1,) + (1,) * (len(shape) - position - 1))

    factor_of = one(*cuts[0])
    for cut in cuts[1:]:
        factor_of = factor_of * one(*cut)
    return factor_of


def centred(stream_key, shape, width, reach, pieces=(), held_as=jnp.bfloat16):
    values = width * jax.random.normal(stream_key, shape, jnp.float32)
    if pieces:
        values = values * steps_of(stream_key, shape, pieces, -0.22, 0.18)
    return jnp.clip(values, -reach, reach).astype(held_as)


def setup_inputs(seed: int = 0) -> dict:
    streams_of = jax.random.split(jax.random.key(seed), 12)
    return {
        "hidden_in": draw_hidden_in(jax.random.fold_in(streams_of[11], 71), 0),
        "cache_keys": draw_cache_keys(jax.random.fold_in(streams_of[11], 71), 0),
        "cache_values": centred(streams_of[2], (REQ, MAXLEN, D), 1.0, 6.0, ((1, 16), (2, 2))),
        "lengths": draw_lengths(jax.random.fold_in(streams_of[11], 71), 0),
        "query_weight": centred(streams_of[4], (D, D), D ** -0.5, 0.125, ((0, 16), (1, 2))),
        "key_weight": centred(streams_of[5], (D, D), D ** -0.5, 0.125, ((0, 16), (1, 2))),
        "value_weight": centred(streams_of[6], (D, D), D ** -0.5, 0.125, ((0, 16), (1, 2))),
        "out_weight": centred(streams_of[7], (D, D), D ** -0.5, 0.125, ((0, 2), (1, 16))),
        "gate_weight": centred(streams_of[8], (D, FF), D ** -0.5, 0.125, ((0, 16), (1, 2))),
        "up_weight": centred(streams_of[9], (D, FF), D ** -0.5, 0.125, ((0, 16), (1, 2))),
        "down_weight": centred(streams_of[10], (FF, D), FF ** -0.5, 0.0625, ((0, 2), (1, 16))),
    }


EPS = 1e-05
THETA = 10000.0
NEGATIVE = -1e+30

def layer_norm(row_block):
    row_mean = lax.optimization_barrier(jnp.mean(row_block, axis=-1, keepdims=True))
    second_moment = lax.optimization_barrier(jnp.mean(row_block * row_block, axis=-1, keepdims=True))
    return (row_block - row_mean) / jnp.sqrt(second_moment - row_mean * row_mean + EPS)

def rotate(vectors, placed_pos):
    half_dim = HEAD_DIM // 2
    freqs = THETA ** (-jnp.arange(half_dim, dtype=jnp.float32) * 2.0 / HEAD_DIM)
    angles = placed_pos.astype(jnp.float32)[..., None, None] * freqs
    cosine = jnp.cos(angles)
    sine = jnp.sin(angles)
    first_half = vectors[..., :half_dim]
    second_half = vectors[..., half_dim:]
    return jnp.concatenate([first_half * cosine - second_half * sine, second_half * cosine + first_half * sine], axis=-1)

def reference(hidden_in, cache_keys, cache_values, lengths, query_weight, key_weight, value_weight, out_weight, gate_weight, up_weight, down_weight):
    widened = hidden_in.astype(jnp.float32)
    normed = layer_norm(widened).astype(jnp.bfloat16).reshape(REQ * NEW, D)
    queries = jnp.dot(normed, query_weight, preferred_element_type=jnp.float32).reshape(REQ, NEW, HEADS, HEAD_DIM)
    new_keys = jnp.dot(normed, key_weight, preferred_element_type=jnp.float32).reshape(REQ, NEW, HEADS, HEAD_DIM)
    new_values = jnp.dot(normed, value_weight, preferred_element_type=jnp.float32).reshape(REQ, NEW, HEADS, HEAD_DIM)
    positions = lengths[:, None] + jnp.arange(NEW, dtype=jnp.int32)[None, :]
    rot_queries = rotate(queries, positions).astype(jnp.bfloat16)
    new_keys = rotate(new_keys, positions).astype(jnp.bfloat16)
    new_values = new_values.astype(jnp.bfloat16)
    score_scale = 1.0 / jnp.sqrt(jnp.float32(HEAD_DIM))

    def attend(items):
        query_rows, key_rows, value_rows, old_keys, old_values, length_one = items
        query_rows = query_rows.astype(jnp.float32)
        old_keys = old_keys.reshape(MAXLEN, HEADS, HEAD_DIM).astype(jnp.float32)
        old_values = old_values.reshape(MAXLEN, HEADS, HEAD_DIM).astype(jnp.float32)
        old_scores = jnp.einsum('thd,jhd->thj', query_rows, old_keys, precision=lax.Precision.HIGHEST) * score_scale
        slot_ids = jnp.arange(MAXLEN, dtype=jnp.int32)
        old_scores = jnp.where(slot_ids[None, None, :] < length_one, old_scores, NEGATIVE)
        new_scores = jnp.einsum('thd,shd->ths', query_rows, key_rows.astype(jnp.float32), precision=lax.Precision.HIGHEST) * score_scale
        token_ids = jnp.arange(NEW, dtype=jnp.int32)
        new_scores = jnp.where(token_ids[None, None, :] <= token_ids[:, None, None], new_scores, NEGATIVE)
        top_score = jnp.maximum(lax.optimization_barrier(jnp.max(old_scores, axis=-1)), lax.optimization_barrier(jnp.max(new_scores, axis=-1)))
        old_weights = jnp.exp(old_scores - top_score[..., None])
        new_weights = jnp.exp(new_scores - top_score[..., None])
        running = lax.optimization_barrier(jnp.sum(old_weights, axis=-1)) + lax.optimization_barrier(jnp.sum(new_weights, axis=-1))
        summed = jnp.einsum('thj,jhd->thd', old_weights, old_values, precision=lax.Precision.HIGHEST)
        summed = summed + jnp.einsum('ths,shd->thd', new_weights, value_rows.astype(jnp.float32), precision=lax.Precision.HIGHEST)
        return (summed / running[..., None]).reshape(NEW, D)
    attended = lax.map(attend, (rot_queries, new_keys, new_values, cache_keys, cache_values, lengths)).astype(jnp.bfloat16)
    mixed = widened + jnp.dot(attended.reshape(REQ * NEW, D), out_weight, preferred_element_type=jnp.float32).reshape(REQ, NEW, D)
    normed2 = layer_norm(mixed).astype(jnp.bfloat16).reshape(REQ * NEW, D)
    gate = jnp.dot(normed2, gate_weight, preferred_element_type=jnp.float32)
    up_rows = jnp.dot(normed2, up_weight, preferred_element_type=jnp.float32)
    act = (jax.nn.silu(gate) * up_rows).astype(jnp.bfloat16)
    hidden_out = (mixed + jnp.dot(act, down_weight, preferred_element_type=jnp.float32).reshape(REQ, NEW, D)).astype(jnp.bfloat16)

    def write_rows(cache_one, rows_one, start_one):
        return lax.dynamic_update_slice(cache_one, rows_one, (start_one.astype(jnp.int32), jnp.int32(0)))
    new_cache_keys = jax.vmap(write_rows)(cache_keys, new_keys.reshape(REQ, NEW, D), lengths)
    new_cache_values = jax.vmap(write_rows)(cache_values, new_values.reshape(REQ, NEW, D), lengths)
    return (hidden_out, new_cache_keys, new_cache_values)
```

```python
import functools
import math

import jax
import jax.numpy as jnp
from jax import lax
from jax.experimental import pallas as pl
from jax.experimental.pallas import tpu as pltpu
from jax.sharding import PartitionSpec as P

D = 2048
HEADS = 16


EPS = 1e-05
THETA = 10000.0
NEGATIVE = -1e30


def rotate(vectors, placed_pos):
    head_size = vectors.shape[-1]
    half_dim = head_size // 2
    freqs = THETA ** (-jnp.arange(half_dim, dtype=jnp.float32) * 2.0 / head_size)
    angles = placed_pos.astype(jnp.float32)[..., None, None] * freqs
    cosine = jnp.cos(angles)
    sine = jnp.sin(angles)
    first_half = vectors[..., :half_dim]
    second_half = vectors[..., half_dim:]
    return jnp.concatenate(
        [first_half * cosine - second_half * sine, second_half * cosine + first_half * sine],
        axis=-1,
    )


def normalize(widened, row_sums, square_sums):
    row_mean = row_sums / D
    second_moment = square_sums / D
    inverse = 1.0 / jnp.sqrt(second_moment - row_mean * row_mean + EPS)
    return ((widened - row_mean[..., None]) * inverse[..., None]).astype(jnp.bfloat16)


def body_plain(
    hidden_in,
    cache_keys,
    cache_values,
    lengths,
    query_weight,
    key_weight,
    value_weight,
    out_weight,
    gate_weight,
    up_weight,
    down_weight,
):
    requests, token_count, narrow_width = hidden_in.shape
    slot_count = cache_keys.shape[1]
    local_width = cache_keys.shape[2]
    head_size = D // HEADS
    local_heads = local_width // head_size
    score_scale = 1.0 / math.sqrt(head_size)
    shard_index = lax.axis_index("seq")
    slot_ids = shard_index * slot_count + jnp.arange(slot_count, dtype=jnp.int32)
    live_slots = slot_ids[None, :] < lengths[:, None]
    old_keys = cache_keys.reshape(requests, slot_count, local_heads, head_size)
    old_values = cache_values.reshape(requests, slot_count, local_heads, head_size).astype(
        jnp.float32
    )
    positions = lengths[:, None] + jnp.arange(token_count, dtype=jnp.int32)[None, :]
    out_list = []
    key_list = []
    value_list = []
    for token_step in range(1):
        row_block = hidden_in
        block_rows = row_block.shape[1]
        widened = row_block.astype(jnp.float32)
        row_sums, square_sums = lax.psum(
            (jnp.sum(widened, axis=-1), jnp.sum(widened * widened, axis=-1)), "seq"
        )
        normed = normalize(widened, row_sums, square_sums)
        query_part = jnp.einsum(
            "rnc,cm->rnm", normed, query_weight, preferred_element_type=jnp.float32
        )
        key_part = jnp.einsum("rnc,cm->rnm", normed, key_weight, preferred_element_type=jnp.float32)
        value_part = jnp.einsum(
            "rnc,cm->rnm", normed, value_weight, preferred_element_type=jnp.float32
        )
        queries, keys_full, values_full = lax.psum((query_part, key_part, value_part), "seq")
        placed_pos = positions[:, token_step : token_step + block_rows]
        queries = rotate(
            queries.reshape(requests, block_rows, local_heads, head_size), placed_pos
        ).astype(jnp.bfloat16)
        new_key = rotate(
            keys_full.reshape(requests, block_rows, local_heads, head_size), placed_pos
        ).astype(jnp.bfloat16)
        new_value = values_full.reshape(requests, block_rows, local_heads, head_size).astype(
            jnp.bfloat16
        )
        keys_new = jnp.concatenate(key_list + [new_key], axis=1)
        values_new = jnp.concatenate(value_list + [new_value], axis=1)
        old_scores = (
            jnp.einsum("rnhd,rjhd->rnhj", queries, old_keys, preferred_element_type=jnp.float32)
            * score_scale
        )
        old_scores = jnp.where(live_slots[:, None, None, :], old_scores, NEGATIVE)
        top_old = jnp.max(old_scores, axis=-1)
        weights_old = jnp.where(
            live_slots[:, None, None, :], jnp.exp(old_scores - top_old[..., None]), 0.0
        )
        total_old = jnp.sum(weights_old, axis=-1)
        summed_old = jnp.einsum(
            "rnhj,rjhd->rnhd", weights_old, old_values, precision=lax.Precision.HIGHEST
        )
        top_cache = lax.pmax(top_old, "seq")
        factor_old = jnp.exp(top_old - top_cache)
        total_cache, summed_cache = lax.psum(
            (total_old * factor_old, summed_old * factor_old[..., None]), "seq"
        )
        new_scores = (
            jnp.einsum("rnhd,rshd->rnhs", queries, keys_new, preferred_element_type=jnp.float32)
            * score_scale
        )
        key_index = jnp.arange(keys_new.shape[1], dtype=jnp.int32)
        query_index = token_step + jnp.arange(block_rows, dtype=jnp.int32)
        allowed = key_index[None, :] <= query_index[:, None]
        new_scores = jnp.where(allowed[None, :, None, :], new_scores, NEGATIVE)
        top_new = jnp.max(new_scores, axis=-1)
        weights_new = jnp.exp(new_scores - top_new[..., None])
        total_new = jnp.sum(weights_new, axis=-1)
        summed_new = jnp.einsum(
            "rnhs,rshd->rnhd",
            weights_new,
            values_new.astype(jnp.float32),
            precision=lax.Precision.HIGHEST,
        )
        top_score = jnp.maximum(top_cache, top_new)
        factor_cache = jnp.exp(top_cache - top_score)
        factor_new = jnp.exp(top_new - top_score)
        running = total_cache * factor_cache + total_new * factor_new
        combined = summed_cache * factor_cache[..., None] + summed_new * factor_new[..., None]
        attended = (
            (combined / running[..., None])
            .astype(jnp.bfloat16)
            .reshape(requests, block_rows, local_width)
        )
        attn_part = jnp.einsum(
            "rnm,mc->rnc", attended, out_weight, preferred_element_type=jnp.float32
        )
        mixed = widened + lax.psum(attn_part, "mdl")
        sums_mixed, squares_mixed = lax.psum(
            (jnp.sum(mixed, axis=-1), jnp.sum(mixed * mixed, axis=-1)), "seq"
        )
        normed2 = normalize(mixed, sums_mixed, squares_mixed)
        gate_part = jnp.einsum(
            "rnc,cf->rnf", normed2, gate_weight, preferred_element_type=jnp.float32
        )
        up_part = jnp.einsum("rnc,cf->rnf", normed2, up_weight, preferred_element_type=jnp.float32)
        gate_full, up_full = lax.psum((gate_part, up_part), "seq")
        act_full = (jax.nn.silu(gate_full) * up_full).astype(jnp.bfloat16)
        down_part = jnp.einsum(
            "rnf,fc->rnc", act_full, down_weight, preferred_element_type=jnp.float32
        )
        block_out = (mixed + lax.psum(down_part, "mdl")).astype(jnp.bfloat16)
        block_out, new_key, new_value = (block_out, new_key, new_value)
        out_list.append(block_out)
        key_list.append(new_key)
        value_list.append(new_value)
    hidden_out = jnp.concatenate(out_list, axis=1)
    keys_all = jnp.concatenate(key_list, axis=1)
    values_all = jnp.concatenate(value_list, axis=1)
    slot_hits = slot_ids[None, None, :] == positions[:, :, None]
    one_hot = slot_hits.astype(jnp.bfloat16)
    written = jnp.any(slot_hits, axis=1)[..., None]
    placed_keys = jnp.einsum(
        "rts,rtm->rsm",
        one_hot,
        keys_all.reshape(requests, token_count, local_width),
        preferred_element_type=jnp.float32,
    ).astype(jnp.bfloat16)
    placed_values = jnp.einsum(
        "rts,rtm->rsm",
        one_hot,
        values_all.reshape(requests, token_count, local_width),
        preferred_element_type=jnp.float32,
    ).astype(jnp.bfloat16)
    new_cache_keys = jnp.where(written, placed_keys, cache_keys)
    new_cache_values = jnp.where(written, placed_values, cache_values)
    return (hidden_out, new_cache_keys, new_cache_values)


PLANE = 4
MESH = pl.DeviceIdType.MESH
F32 = jnp.float32
BF16 = jnp.bfloat16
SEMS = 208


def flip(value, mask):
    out = value
    for b in range(4):
        if mask >> b & 1:
            out = out + (1 - 2 * (value // (1 << b) % 2)) * (1 << b)
    return out


class Links:
    def __init__(self, send, recv):
        self.send, self.recv, self.used, self.all = send, recv, 0, []

    def post(self, src, dst, device):
        i = self.used
        self.used += 1
        copy = pltpu.make_async_remote_copy(
            src_ref=src,
            dst_ref=dst,
            send_sem=self.send.at[i],
            recv_sem=self.recv.at[i],
            device_id=device,
            device_id_type=MESH,
        )
        copy.start()
        self.all.append(copy)
        return copy


def wait_all(copies):
    for copy in copies:
        copy.wait()


def to_lanes(columns):
    rows = columns.shape[0]
    if rows < 128:
        columns = jnp.concatenate([columns, jnp.zeros((128 - rows, 128), F32)], axis=0)
    return columns.T


def pack_sums(widened):
    rows = widened.shape[0]
    lanes = lax.broadcasted_iota(jnp.int32, (rows, 128), 1)
    first = jnp.sum(widened, axis=-1, keepdims=True)
    second = jnp.sum(widened * widened, axis=-1, keepdims=True)
    return to_lanes(jnp.where(lanes == 0, first, jnp.where(lanes == 1, second, 0.0)))[0:8]


def moments(slots, n, rows):
    total = slots[0]
    for i in range(1, n):
        total = total + slots[i]
    back = jnp.concatenate([total, jnp.zeros((120, 128), F32)], axis=0).T[0:rows]
    mean = back[:, 0:1] / D
    inverse = 1.0 / jnp.sqrt(back[:, 1:2] / D - mean * mean + EPS)
    return mean, inverse


def layer_kernel(
    n,
    scale,
    lens,
    x_hbm,
    wq,
    wk,
    wv,
    ck_hbm,
    cv_hbm,
    wo_hbm,
    wg,
    wu,
    wd,
    out_ref,
    kv_all,
    xs,
    ck,
    cv,
    wo,
    wqkv_r,
    wg_r,
    wu_r,
    wd_r,
    stat1,
    x_all,
    q_part,
    q_got,
    kv_part,
    kv_got,
    q_all,
    acc_part,
    acc_got,
    st_part,
    st_got,
    att_all,
    o_mine,
    o_other,
    mixed_all,
    stat2,
    normed2,
    gu_mine,
    gu_send,
    gu_got,
    d_mine,
    d_other,
    d_send,
    d_got,
    send,
    recv,
    local,
):
    me = lax.axis_index("seq")
    core = lax.axis_index("mdl")
    z, p = me // PLANE, me % PLANE
    g = me % 8
    links = Links(send, recv)
    partner = {"mdl": 1 - core}
    slots = ck.shape[1]
    ff = wg_r.shape[2]
    loads = {}

    def load(name, src, dst):
        copy = pltpu.make_async_copy(src, dst, local.at[len(loads)])
        copy.start()
        loads[name] = copy

    def peer(k):
        return {"seq": flip(me, k)}

    load("x", x_hbm, xs)
    barrier = pltpu.get_barrier_semaphore()
    for k in range(1, n):
        pl.semaphore_signal(barrier, inc=1, device_id=peer(k), device_id_type=MESH)
    pl.semaphore_signal(barrier, inc=1, device_id=partner, device_id_type=MESH)

    def cols(ref, index, width):
        return ref.at[:, pl.ds(pl.multiple_of(index * width, width), width)]

    def rows_of(ref, index, height):
        return ref.at[pl.ds(pl.multiple_of(index * height, height), height)]

    for i, w in enumerate((wq, wk, wv)):
        load(("w", i), cols(w, p, 256), wqkv_r.at[i, p])
    load("k", ck_hbm, ck)
    load("v", cv_hbm, cv)
    load("o", wo_hbm, wo)
    load("g", cols(wg, g, ff), wg_r.at[g])
    load("u", cols(wu, g, ff), wu_r.at[g])
    load("d", rows_of(wd, g, ff), wd_r.at[g])

    loads["x"].wait()
    widened = xs[...].astype(F32)
    stat1[me] = pack_sums(widened)
    pl.semaphore_wait(barrier, n)

    flying = [links.post(stat1.at[me], stat1.at[me], peer(k)) for k in range(1, n)]
    x_fly = [links.post(xs, x_all.at[j - 1], peer(j)) for j in (1, 2, 3)]
    w_fly = [
        [
            links.post(cols(w, flip(p, j), 256), wqkv_r.at[i, p], peer(j))
            for j in (1, 2, 3)
        ]
        for i, w in enumerate((wq, wk, wv))
    ]

    order = (1, 2, 4, 3, 5, 6, 7)
    piece = ff // 2

    def gate_round(w, held, half):
        def start():
            return [
                links.post(
                    w.at[:, pl.ds(pl.multiple_of(flip(g, k) * ff + half * piece, piece), piece)],
                    held.at[g, :, half * piece : (half + 1) * piece],
                    peer(k),
                )
                for k in order
            ]

        return start

    def down_round(half):
        def start():
            return [
                links.post(
                    wd.at[pl.ds(pl.multiple_of(flip(g, k) * ff + half * piece, piece), piece)],
                    wd_r.at[g, half * piece : (half + 1) * piece],
                    peer(k),
                )
                for k in order
            ]

        return start

    row = lax.broadcasted_iota(jnp.int32, (32, 128), 0)
    lane = lax.broadcasted_iota(jnp.int32, (32, 128), 1)
    position = row % 4
    for i in range(8):
        position = position + jnp.where(row // 4 == i, lens[z * 8 + i], 0)
    freqs = jnp.exp((lane % 64).astype(F32) * (-2.0 / 128 * math.log(THETA)))
    angles = position.astype(F32) * freqs
    cosine = jnp.cos(angles)
    sine = jnp.where(lane < 64, -jnp.sin(angles), jnp.sin(angles))

    wait_all(flying)
    mean, inverse = moments(stat1, n, 128)
    wait_all(x_fly)

    def block_of(j):
        held = xs[...] if j == 0 else x_all[j - 1]
        return ((held.astype(F32) - mean) * inverse).astype(BF16)

    blocks = [block_of(j) for j in range(4)]

    def project(i):
        loads["w", i].wait()
        wait_all(w_fly[i])
        made = jnp.dot(blocks[0], wqkv_r[i, p], preferred_element_type=F32)
        for j in range(1, 4):
            made = made + jnp.dot(blocks[j], wqkv_r[i, flip(p, j)], preferred_element_type=F32)
        return made.reshape(PLANE, 32, 256)

    def rotate_rows(sums):
        return jnp.concatenate(
            [
                sums[:, i * 128 : (i + 1) * 128] * cosine
                + pltpu.roll(sums[:, i * 128 : (i + 1) * 128], 64, 1) * sine
                for i in range(2)
            ],
            axis=1,
        ).astype(BF16)

    q_part[...] = project(0)
    q_fly = [links.post(q_part.at[flip(z, i)], q_got.at[i - 1], peer(4 * i)) for i in (1, 2, 3)]
    for i in (1, 2):
        kv_part[:, i - 1] = project(i).astype(BF16)
    wait_all(q_fly)
    sums = q_part[z]
    for i in range(3):
        sums = sums + q_got[i]
    q_all[z, p] = rotate_rows(sums)
    q_fly = {k: links.post(q_all.at[z, p], q_all.at[z, p], peer(k)) for k in range(1, n)}
    kv_fly = [
        links.post(kv_part.at[flip(z, i)], kv_got.at[i - 1], peer(4 * i)) for i in (1, 2, 3)
    ]
    bulk_1 = gate_round(wg, wg_r, 0)()

    loads["k"].wait()
    loads["v"].wait()
    row16 = lax.broadcasted_iota(jnp.int32, (16, 128), 0)
    lane16 = lax.broadcasted_iota(jnp.int32, (16, 128), 1)
    slot = me * slots + lane16 % 32
    acc_fly, st_fly = {}, {}
    for i in range(4):
        zb = flip(z, i)
        for j in range(4):
            if 4 * i + j:
                q_fly[4 * i + j].wait()
        packs = []
        for half in range(2):
            first = zb * 8 + half * 4
            length = jnp.where(lane16 // 32 == 0, lens[first], 0)
            for a in range(1, 4):
                length = jnp.where(lane16 // 32 == a, lens[first + a], length)
            live = (row16 // 4 == lane16 // 32) & (slot < length)
            rows = slice(half * 16, half * 16 + 16)
            pack = jnp.zeros((16, 128), F32)
            for h in range(8):
                head = slice(h * 128, (h + 1) * 128)
                part = slice(h % 2 * 128, h % 2 * 128 + 128)
                keys = ck[pl.ds(first, 4), :, head].reshape(128, 128)
                values = cv[pl.ds(first, 4), :, head].reshape(128, 128)
                scores = (
                    lax.dot_general(
                        q_all[zb, h // 2, rows, part],
                        keys,
                        (((1,), (1,)), ((), ())),
                        preferred_element_type=F32,
                    )
                    * scale
                )
                scores = jnp.where(live, scores, NEGATIVE)
                top = jnp.max(scores, axis=-1, keepdims=True)
                weights = jnp.where(live, jnp.exp(scores - top), 0.0)
                total = jnp.sum(weights, axis=-1, keepdims=True)
                coarse = weights.astype(BF16)
                fine = (weights - coarse.astype(F32)).astype(BF16)
                both = jnp.dot(
                    jnp.concatenate([coarse, fine], axis=0), values, preferred_element_type=F32
                )
                acc_part[i, h // 2, rows, part] = (both[0:16] + both[16:32]).astype(BF16)
                at = 8 * (h // 2) + h % 2
                pack = jnp.where(lane16 == at, top, jnp.where(lane16 == at + 2, total, pack))
            packs.append(pack)
        turned = to_lanes(jnp.concatenate(packs, axis=0))
        for q in range(4):
            st_part[i, q] = turned[8 * q : 8 * q + 8]
        for j in range(4):
            k = 4 * i + j
            if k:
                st_fly[k] = links.post(st_part.at[i, flip(p, j)], st_got.at[k - 1], peer(k))
                acc_fly[k] = links.post(acc_part.at[i, flip(p, j)], acc_got.at[k - 1], peer(k))
    bulk_2 = gate_round(wu, wu_r, 0)()

    wait_all(kv_fly)
    sums_k, sums_v = kv_part[z, 0].astype(F32), kv_part[z, 1].astype(F32)
    for i in range(3):
        sums_k = sums_k + kv_got[i, 0].astype(F32)
        sums_v = sums_v + kv_got[i, 1].astype(F32)
    kv_all[z, p, 0] = rotate_rows(sums_k)
    kv_all[z, p, 1] = sums_v.astype(BF16)
    token = lax.broadcasted_iota(jnp.int32, (32, 32), 0)
    key = lax.broadcasted_iota(jnp.int32, (32, 32), 1)
    allowed = (token // 4 == key // 4) & (key <= token)
    fresh = []
    for j in range(2):
        part = slice(j * 128, (j + 1) * 128)
        scores = (
            lax.dot_general(
                q_all[z, p, :, part],
                kv_all[z, p, 0, :, part],
                (((1,), (1,)), ((), ())),
                preferred_element_type=F32,
            )
            * scale
        )
        fresh.append(jnp.where(allowed, scores, NEGATIVE))

    for k in range(1, n):
        st_fly[k].wait()
    tiles = [st_part[0, p]] + [st_got[k - 1] for k in range(1, n)]
    top = tiles[0]
    for tile in tiles[1:]:
        top = jnp.maximum(top, tile)
    factors = [jnp.exp(tile - top) for tile in tiles]
    total = pltpu.roll(tiles[0], 6, 0) * factors[0]
    for tile, factor in zip(tiles[1:], factors[1:]):
        total = total + pltpu.roll(tile, 6, 0) * factor
    sub = lax.broadcasted_iota(jnp.int32, (8, 128), 0)
    factors[0] = jnp.where(
        sub < 2,
        factors[0],
        jnp.where(sub < 4, pltpu.roll(top, 2, 0), pltpu.roll(total, 4, 0)),
    )
    back = jnp.concatenate(factors, axis=0).T[0:32]
    for k in range(1, n):
        acc_fly[k].wait()
    for j in range(2):
        part = slice(j * 128, (j + 1) * 128)
        summed = acc_part[0, p, :, part].astype(F32) * back[:, j : j + 1]
        for k in range(1, n):
            summed = summed + acc_got[k - 1, :, part].astype(F32) * back[:, 8 * k + j : 8 * k + j + 1]
        top_cache, total_cache = back[:, 2 + j : 3 + j], back[:, 4 + j : 5 + j]
        scores = fresh[j]
        top_all = jnp.maximum(top_cache, jnp.max(scores, axis=-1, keepdims=True))
        weights = jnp.where(allowed, jnp.exp(scores - top_all), 0.0)
        kept = jnp.exp(top_cache - top_all)
        running = total_cache * kept + jnp.sum(weights, axis=-1, keepdims=True)
        summed = summed * kept + jnp.dot(
            weights,
            kv_all[z, p, 1, :, part].astype(F32),
            precision=lax.Precision.HIGHEST,
            preferred_element_type=F32,
        )
        att_all[z, p, :, part] = (summed / running).astype(BF16)
    att_fly = {k: links.post(att_all.at[z, p], att_all.at[z, p], peer(k)) for k in range(1, n)}
    bulk_1 += gate_round(wg, wg_r, 1)()

    loads["o"].wait()
    for i in range(4):
        zb = flip(z, i)
        for j in range(4):
            if 4 * i + j:
                att_fly[4 * i + j].wait()
        attended = jnp.concatenate([att_all[zb, q] for q in range(4)], axis=1)
        o_mine[zb] = jnp.dot(attended, wo[...], preferred_element_type=F32)
    swap = links.post(o_mine.at[pl.ds(2 * (1 - core), 2)], o_other, partner)
    bulk_2 += gate_round(wu, wu_r, 1)()
    swap.wait()
    mixed = xs[pl.ds(pl.multiple_of(core * 64, 64), 64)].astype(F32) + (
        o_mine[pl.ds(2 * core, 2)] + o_other[...]
    ).reshape(64, 128)
    mixed_all[g] = mixed
    stat2[me] = pack_sums(mixed)
    flying = [links.post(stat2.at[me], stat2.at[me], peer(k)) for k in range(1, n)]
    mix_fly = [links.post(mixed_all.at[g], mixed_all.at[g], peer(k)) for k in range(1, 8)]
    kv_fly = [links.post(kv_all.at[z, p], kv_all.at[z, p], peer(4 * i)) for i in (1, 2, 3)]
    wait_all(flying)
    mean, inverse = moments(stat2, n, 64)
    wait_all(mix_fly)
    for i in range(8):
        normed2[core, :, i * 128 : (i + 1) * 128] = (
            (mixed_all[i] - mean) * inverse
        ).astype(BF16)
    swap = links.post(normed2.at[core], normed2.at[core], partner)
    loads["g"].wait()
    loads["u"].wait()
    wait_all(bulk_1)
    swap.wait()
    rows = normed2[...].reshape(128, 1024)
    chunks = gu_mine.shape[0]
    tile = ff // chunks
    gu_fly = []
    for c in range(chunks):
        here = slice(c * tile, (c + 1) * tile)
        gate = jnp.dot(rows, wg_r[:, :, here].reshape(1024, tile), preferred_element_type=F32)
        if c == 0:
            wait_all(bulk_2)
        up = jnp.dot(rows, wu_r[:, :, here].reshape(1024, tile), preferred_element_type=F32)
        gu_mine[c, 0] = gate
        gu_mine[c, 1] = up
        gu_send[c, 0] = gate.astype(BF16)
        gu_send[c, 1] = up.astype(BF16)
        gu_fly.append(links.post(gu_send.at[c], gu_got.at[c], peer(8)))
    bulk_3 = down_round(0)() + down_round(1)()
    wait_all(kv_fly)
    kv_fly = [
        links.post(kv_all.at[:, p], kv_all.at[:, p], peer(j)) for j in (1, 2, 3)
    ]
    loads["d"].wait()
    for c in range(chunks):
        here = slice(c * tile, (c + 1) * tile)
        gu_fly[c].wait()
        gate = gu_mine[c, 0] + gu_got[c, 0].astype(F32)
        up = gu_mine[c, 1] + gu_got[c, 1].astype(F32)
        act = (gate / (1.0 + jnp.exp(-gate)) * up).astype(BF16)
        if c == 0:
            wait_all(bulk_3)
        for i in range(8):
            made = jnp.dot(act, wd_r[i, here], preferred_element_type=F32).reshape(2, 64, 128)
            d_mine[:, i] = made if c == 0 else d_mine[:, i] + made
    swap = links.post(d_mine.at[1 - core], d_other, partner)
    swap.wait()
    sums = d_mine[core] + d_other[...]
    d_send[...] = sums.astype(BF16)
    d_mine[core] = sums
    flying = [links.post(d_send.at[flip(g, k)], d_got.at[k - 1], peer(k)) for k in range(1, 8)]
    wait_all(flying)
    total = d_mine[core, g]
    for k in range(7):
        total = total + d_got[k].astype(F32)
    out_ref[core] = (mixed_all[g] + total).astype(BF16)
    swap = links.post(out_ref.at[core], out_ref.at[core], partner)
    swap.wait()
    wait_all(kv_fly)


def write_kernel(lens, hidden, kv_ref, k_ref, v_ref, out_ref, ko_ref, vo_ref):
    step = pl.program_id(0)
    group, slots, width = k_ref.shape
    base = lax.axis_index("seq") * slots

    @pl.when(step == 0)
    def _():
        out_ref[...] = hidden[...].reshape(out_ref.shape)

    ko_ref[...] = k_ref[...]
    vo_ref[...] = v_ref[...]
    for i in range(group):
        first = lens[step * group + i] - base

        @pl.when((first < slots) & (first > -4))
        def _():
            place = lax.broadcasted_iota(jnp.int32, (slots, 256), 0)
            for c, old, out in ((0, k_ref, ko_ref), (1, v_ref, vo_ref)):
                for q in range(4):
                    part = slice(q * 256, (q + 1) * 256)
                    fresh = kv_ref[step, q, c].astype(F32)[4 * i : 4 * i + 4]
                    held = old[i, :, part].astype(F32)
                    for t in range(4):
                        held = jnp.where(place == first + t, fresh[t : t + 1], held)
                    out[i, :, part] = held.astype(BF16)


def body_kernels(
    n,
    hidden_in,
    cache_keys,
    cache_values,
    lengths,
    query_weight,
    key_weight,
    value_weight,
    out_weight,
    gate_weight,
    up_weight,
    down_weight,
):
    requests, token_count, narrow = hidden_in.shape
    rows = requests * token_count
    slot_count, local_width = cache_keys.shape[1:]
    score_scale = 1.0 / math.sqrt(D // HEADS)
    ff = gate_weight.shape[1] // 8
    chunks = 2
    struct = jax.ShapeDtypeStruct
    vmem = pl.BlockSpec(memory_space=pltpu.VMEM)
    smem = pl.BlockSpec(memory_space=pltpu.SMEM)
    far = pl.BlockSpec(memory_space=pltpu.HBM)
    hidden_out, kv_all = pl.pallas_call(
        functools.partial(layer_kernel, n, score_scale),
        out_shape=[
            struct((2, rows // 2, narrow), BF16),
            struct((4, PLANE, 2, 32, 256), BF16),
        ],
        in_specs=[smem] + [far] * 10,
        out_specs=[vmem, vmem],
        scratch_shapes=[
            pltpu.VMEM((rows, narrow), BF16),
            pltpu.VMEM((requests, slot_count, local_width), BF16),
            pltpu.VMEM((requests, slot_count, local_width), BF16),
            pltpu.VMEM((local_width, narrow), BF16),
            pltpu.VMEM((3, PLANE, narrow, 256), BF16),
            pltpu.VMEM((8, narrow, ff), BF16),
            pltpu.VMEM((8, narrow, ff), BF16),
            pltpu.VMEM((8, ff, narrow), BF16),
            pltpu.VMEM((n, 8, 128), F32),
            pltpu.VMEM((3, rows, narrow), BF16),
            pltpu.VMEM((4, 32, 256), F32),
            pltpu.VMEM((3, 32, 256), F32),
            pltpu.VMEM((4, 2, 32, 256), BF16),
            pltpu.VMEM((3, 2, 32, 256), BF16),
            pltpu.VMEM((4, PLANE, 32, 256), BF16),
            pltpu.VMEM((4, PLANE, 32, 256), BF16),
            pltpu.VMEM((n - 1, 32, 256), BF16),
            pltpu.VMEM((4, PLANE, 8, 128), F32),
            pltpu.VMEM((n - 1, 8, 128), F32),
            pltpu.VMEM((4, PLANE, 32, 256), BF16),
            pltpu.VMEM((4, 32, narrow), F32),
            pltpu.VMEM((2, 32, narrow), F32),
            pltpu.VMEM((8, rows // 2, narrow), F32),
            pltpu.VMEM((n, 8, 128), F32),
            pltpu.VMEM((2, rows // 2, 8 * narrow), BF16),
            pltpu.VMEM((chunks, 2, rows, ff // chunks), F32),
            pltpu.VMEM((chunks, 2, rows, ff // chunks), BF16),
            pltpu.VMEM((chunks, 2, rows, ff // chunks), BF16),
            pltpu.VMEM((2, 8, rows // 2, narrow), F32),
            pltpu.VMEM((8, rows // 2, narrow), F32),
            pltpu.VMEM((8, rows // 2, narrow), BF16),
            pltpu.VMEM((7, rows // 2, narrow), BF16),
            pltpu.SemaphoreType.DMA((SEMS,)),
            pltpu.SemaphoreType.DMA((SEMS,)),
            pltpu.SemaphoreType.DMA((10,)),
        ],
        compiler_params=pltpu.CompilerParams(
            collective_id=1, has_side_effects=True, vmem_limit_bytes=48 * 2**20
        ),
    )(
        lengths,
        hidden_in.reshape(rows, narrow),
        query_weight,
        key_weight,
        value_weight,
        cache_keys,
        cache_values,
        out_weight,
        gate_weight,
        up_weight,
        down_weight,
    )
    group = 8
    block = pl.BlockSpec((group, slot_count, local_width), lambda s: (s, 0, 0))
    return pl.pallas_call(
        write_kernel,
        grid=(requests // group,),
        out_shape=[
            struct(hidden_in.shape, BF16),
            struct(cache_keys.shape, BF16),
            struct(cache_values.shape, BF16),
        ],
        in_specs=[smem, vmem, vmem, block, block],
        out_specs=[pl.BlockSpec(hidden_in.shape, lambda s: (0, 0, 0)), block, block],
    )(lengths, hidden_out, kv_all, cache_keys, cache_values)


def body(n, model_shards, hidden_in, cache_keys, *rest):
    rows = hidden_in.shape[0] * hidden_in.shape[1]
    tiled = (
        n == 16
        and rows == 128
        and hidden_in.shape[1] == 4
        and hidden_in.shape[2] == 128
        and cache_keys.shape[1] == 32
        and cache_keys.shape[2] == 1024
        and model_shards == 2
    )
    if tiled:
        return body_kernels(n, hidden_in, cache_keys, *rest)
    return body_plain(hidden_in, cache_keys, *rest)


def solution(mesh):
    placed = (
        P(None, None, "seq"),
        P(None, "seq", "mdl"),
        P(None, "seq", "mdl"),
        P(),
        P("seq", "mdl"),
        P("seq", "mdl"),
        P("seq", "mdl"),
        P("mdl", "seq"),
        P("seq", "mdl"),
        P("seq", "mdl"),
        P("mdl", "seq"),
    )
    return jax.shard_map(
        functools.partial(body, mesh.shape["seq"], mesh.shape["mdl"]),
        mesh=mesh,
        in_specs=placed,
        out_specs=(P(None, None, "seq"), P(None, "seq", "mdl"), P(None, "seq", "mdl")),
        check_vma=False,
    )
```

```python
import functools
import math

import jax
import jax.numpy as jnp
from jax import lax
from jax.experimental import pallas as pl
from jax.experimental.pallas import tpu as pltpu
from jax.sharding import PartitionSpec as P

D = 2048
HEADS = 16


EPS = 1e-05
THETA = 10000.0
NEGATIVE = -1e30


def rotate(vectors, placed_pos):
    head_size = vectors.shape[-1]
    half_dim = head_size // 2
    freqs = THETA ** (-jnp.arange(half_dim, dtype=jnp.float32) * 2.0 / head_size)
    angles = placed_pos.astype(jnp.float32)[..., None, None] * freqs
    cosine = jnp.cos(angles)
    sine = jnp.sin(angles)
    first_half = vectors[..., :half_dim]
    second_half = vectors[..., half_dim:]
    return jnp.concatenate(
        [first_half * cosine - second_half * sine, second_half * cosine + first_half * sine],
        axis=-1,
    )


def normalize(widened, row_sums, square_sums):
    row_mean = row_sums / D
    second_moment = square_sums / D
    inverse = 1.0 / jnp.sqrt(second_moment - row_mean * row_mean + EPS)
    return ((widened - row_mean[..., None]) * inverse[..., None]).astype(jnp.bfloat16)


def body_plain(
    hidden_in,
    cache_keys,
    cache_values,
    lengths,
    query_weight,
    key_weight,
    value_weight,
    out_weight,
    gate_weight,
    up_weight,
    down_weight,
):
    requests, token_count, narrow_width = hidden_in.shape
    slot_count = cache_keys.shape[1]
    local_width = cache_keys.shape[2]
    head_size = D // HEADS
    local_heads = local_width // head_size
    score_scale = 1.0 / math.sqrt(head_size)
    shard_index = lax.axis_index("seq")
    slot_ids = shard_index * slot_count + jnp.arange(slot_count, dtype=jnp.int32)
    live_slots = slot_ids[None, :] < lengths[:, None]
    old_keys = cache_keys.reshape(requests, slot_count, local_heads, head_size)
    old_values = cache_values.reshape(requests, slot_count, local_heads, head_size).astype(
        jnp.float32
    )
    positions = lengths[:, None] + jnp.arange(token_count, dtype=jnp.int32)[None, :]
    out_list = []
    key_list = []
    value_list = []
    for token_step in range(1):
        row_block = hidden_in
        block_rows = row_block.shape[1]
        widened = row_block.astype(jnp.float32)
        row_sums, square_sums = lax.psum(
            (jnp.sum(widened, axis=-1), jnp.sum(widened * widened, axis=-1)), "seq"
        )
        normed = normalize(widened, row_sums, square_sums)
        query_part = jnp.einsum(
            "rnc,cm->rnm", normed, query_weight, preferred_element_type=jnp.float32
        )
        key_part = jnp.einsum("rnc,cm->rnm", normed, key_weight, preferred_element_type=jnp.float32)
        value_part = jnp.einsum(
            "rnc,cm->rnm", normed, value_weight, preferred_element_type=jnp.float32
        )
        queries, keys_full, values_full = lax.psum((query_part, key_part, value_part), "seq")
        placed_pos = positions[:, token_step : token_step + block_rows]
        queries = rotate(
            queries.reshape(requests, block_rows, local_heads, head_size), placed_pos
        ).astype(jnp.bfloat16)
        new_key = rotate(
            keys_full.reshape(requests, block_rows, local_heads, head_size), placed_pos
        ).astype(jnp.bfloat16)
        new_value = values_full.reshape(requests, block_rows, local_heads, head_size).astype(
            jnp.bfloat16
        )
        keys_new = jnp.concatenate(key_list + [new_key], axis=1)
        values_new = jnp.concatenate(value_list + [new_value], axis=1)
        old_scores = (
            jnp.einsum("rnhd,rjhd->rnhj", queries, old_keys, preferred_element_type=jnp.float32)
            * score_scale
        )
        old_scores = jnp.where(live_slots[:, None, None, :], old_scores, NEGATIVE)
        top_old = jnp.max(old_scores, axis=-1)
        weights_old = jnp.where(
            live_slots[:, None, None, :], jnp.exp(old_scores - top_old[..., None]), 0.0
        )
        total_old = jnp.sum(weights_old, axis=-1)
        summed_old = jnp.einsum(
            "rnhj,rjhd->rnhd", weights_old, old_values, precision=lax.Precision.HIGHEST
        )
        top_cache = lax.pmax(top_old, "seq")
        factor_old = jnp.exp(top_old - top_cache)
        total_cache, summed_cache = lax.psum(
            (total_old * factor_old, summed_old * factor_old[..., None]), "seq"
        )
        new_scores = (
            jnp.einsum("rnhd,rshd->rnhs", queries, keys_new, preferred_element_type=jnp.float32)
            * score_scale
        )
        key_index = jnp.arange(keys_new.shape[1], dtype=jnp.int32)
        query_index = token_step + jnp.arange(block_rows, dtype=jnp.int32)
        allowed = key_index[None, :] <= query_index[:, None]
        new_scores = jnp.where(allowed[None, :, None, :], new_scores, NEGATIVE)
        top_new = jnp.max(new_scores, axis=-1)
        weights_new = jnp.exp(new_scores - top_new[..., None])
        total_new = jnp.sum(weights_new, axis=-1)
        summed_new = jnp.einsum(
            "rnhs,rshd->rnhd",
            weights_new,
            values_new.astype(jnp.float32),
            precision=lax.Precision.HIGHEST,
        )
        top_score = jnp.maximum(top_cache, top_new)
        factor_cache = jnp.exp(top_cache - top_score)
        factor_new = jnp.exp(top_new - top_score)
        running = total_cache * factor_cache + total_new * factor_new
        combined = summed_cache * factor_cache[..., None] + summed_new * factor_new[..., None]
        attended = (
            (combined / running[..., None])
            .astype(jnp.bfloat16)
            .reshape(requests, block_rows, local_width)
        )
        attn_part = jnp.einsum(
            "rnm,mc->rnc", attended, out_weight, preferred_element_type=jnp.float32
        )
        mixed = widened + lax.psum(attn_part, "mdl")
        sums_mixed, squares_mixed = lax.psum(
            (jnp.sum(mixed, axis=-1), jnp.sum(mixed * mixed, axis=-1)), "seq"
        )
        normed2 = normalize(mixed, sums_mixed, squares_mixed)
        gate_part = jnp.einsum(
            "rnc,cf->rnf", normed2, gate_weight, preferred_element_type=jnp.float32
        )
        up_part = jnp.einsum("rnc,cf->rnf", normed2, up_weight, preferred_element_type=jnp.float32)
        gate_full, up_full = lax.psum((gate_part, up_part), "seq")
        act_full = (jax.nn.silu(gate_full) * up_full).astype(jnp.bfloat16)
        down_part = jnp.einsum(
            "rnf,fc->rnc", act_full, down_weight, preferred_element_type=jnp.float32
        )
        block_out = (mixed + lax.psum(down_part, "mdl")).astype(jnp.bfloat16)
        block_out, new_key, new_value = (block_out, new_key, new_value)
        out_list.append(block_out)
        key_list.append(new_key)
        value_list.append(new_value)
    hidden_out = jnp.concatenate(out_list, axis=1)
    keys_all = jnp.concatenate(key_list, axis=1)
    values_all = jnp.concatenate(value_list, axis=1)
    slot_hits = slot_ids[None, None, :] == positions[:, :, None]
    one_hot = slot_hits.astype(jnp.bfloat16)
    written = jnp.any(slot_hits, axis=1)[..., None]
    placed_keys = jnp.einsum(
        "rts,rtm->rsm",
        one_hot,
        keys_all.reshape(requests, token_count, local_width),
        preferred_element_type=jnp.float32,
    ).astype(jnp.bfloat16)
    placed_values = jnp.einsum(
        "rts,rtm->rsm",
        one_hot,
        values_all.reshape(requests, token_count, local_width),
        preferred_element_type=jnp.float32,
    ).astype(jnp.bfloat16)
    new_cache_keys = jnp.where(written, placed_keys, cache_keys)
    new_cache_values = jnp.where(written, placed_values, cache_values)
    return (hidden_out, new_cache_keys, new_cache_values)


PLANE = 4
MESH = pl.DeviceIdType.MESH
F32 = jnp.float32
BF16 = jnp.bfloat16
SEMS = 208


def flip(value, mask):
    out = value
    for b in range(4):
        if mask >> b & 1:
            out = out + (1 - 2 * (value // (1 << b) % 2)) * (1 << b)
    return out


class Links:
    def __init__(self, send, recv):
        self.send, self.recv, self.used, self.all = send, recv, 0, []

    def post(self, src, dst, device):
        i = self.used
        self.used += 1
        copy = pltpu.make_async_remote_copy(
            src_ref=src,
            dst_ref=dst,
            send_sem=self.send.at[i],
            recv_sem=self.recv.at[i],
            device_id=device,
            device_id_type=MESH,
        )
        copy.start()
        self.all.append(copy)
        return copy


def wait_all(copies):
    for copy in copies:
        copy.wait()


def to_lanes(columns):
    rows = columns.shape[0]
    if rows < 128:
        columns = jnp.concatenate([columns, jnp.zeros((128 - rows, 128), F32)], axis=0)
    return columns.T


def pack_sums(widened):
    rows = widened.shape[0]
    lanes = lax.broadcasted_iota(jnp.int32, (rows, 128), 1)
    first = jnp.sum(widened, axis=-1, keepdims=True)
    second = jnp.sum(widened * widened, axis=-1, keepdims=True)
    return to_lanes(jnp.where(lanes == 0, first, jnp.where(lanes == 1, second, 0.0)))[0:8]


def moments(slots, n, rows):
    total = slots[0]
    for i in range(1, n):
        total = total + slots[i]
    back = jnp.concatenate([total, jnp.zeros((120, 128), F32)], axis=0).T[0:rows]
    mean = back[:, 0:1] / D
    inverse = 1.0 / jnp.sqrt(back[:, 1:2] / D - mean * mean + EPS)
    return mean, inverse


def layer_kernel(
    n,
    scale,
    lens,
    x_hbm,
    wq,
    wk,
    wv,
    ck_hbm,
    cv_hbm,
    wo_hbm,
    wg,
    wu,
    wd,
    out_ref,
    kv_all,
    xs,
    ck,
    cv,
    wo,
    wqkv_r,
    wg_r,
    wu_r,
    wd_r,
    stat1,
    x_all,
    q_part,
    q_got,
    kv_part,
    kv_got,
    q_all,
    acc_part,
    acc_got,
    st_part,
    st_got,
    att_all,
    o_mine,
    o_other,
    mixed_all,
    stat2,
    normed2,
    gu_mine,
    gu_send,
    gu_got,
    d_mine,
    d_other,
    d_send,
    d_got,
    send,
    recv,
    local,
):
    me = lax.axis_index("seq")
    core = lax.axis_index("mdl")
    z, p = me // PLANE, me % PLANE
    g = me % 8
    links = Links(send, recv)
    partner = {"mdl": 1 - core}
    slots = ck.shape[1]
    ff = wg_r.shape[2]
    loads = {}

    def load(name, src, dst):
        copy = pltpu.make_async_copy(src, dst, local.at[len(loads)])
        copy.start()
        loads[name] = copy

    def peer(k):
        return {"seq": flip(me, k)}

    load("x", x_hbm, xs)
    barrier = pltpu.get_barrier_semaphore()
    for k in range(1, n):
        pl.semaphore_signal(barrier, inc=1, device_id=peer(k), device_id_type=MESH)
    pl.semaphore_signal(barrier, inc=1, device_id=partner, device_id_type=MESH)

    def cols(ref, index, width):
        return ref.at[:, pl.ds(pl.multiple_of(index * width, width), width)]

    def rows_of(ref, index, height):
        return ref.at[pl.ds(pl.multiple_of(index * height, height), height)]

    for i, w in enumerate((wq, wk, wv)):
        load(("w", i), cols(w, p, 256), wqkv_r.at[i, p])
    load("k", ck_hbm, ck)
    load("v", cv_hbm, cv)
    load("o", wo_hbm, wo)
    load("g", cols(wg, g, ff), wg_r.at[g])
    load("u", cols(wu, g, ff), wu_r.at[g])
    load("d", rows_of(wd, g, ff), wd_r.at[g])

    loads["x"].wait()
    widened = xs[...].astype(F32)
    stat1[me] = pack_sums(widened)
    pl.semaphore_wait(barrier, n)

    flying = [links.post(stat1.at[me], stat1.at[me], peer(k)) for k in range(1, n)]
    x_fly = [links.post(xs, x_all.at[j - 1], peer(j)) for j in (1, 2, 3)]
    w_fly = [
        [
            links.post(cols(w, flip(p, j), 256), wqkv_r.at[i, p], peer(j))
            for j in (1, 2, 3)
        ]
        for i, w in enumerate((wq, wk, wv))
    ]

    pieces = {"g": [], "u": [], "d": []}

    def give(name, *masks):
        for k in masks:
            if name == "d":
                src, dst = rows_of(wd, flip(g, k), ff), wd_r.at[g]
            else:
                w, held = (wg, wg_r) if name == "g" else (wu, wu_r)
                src, dst = cols(w, flip(g, k), ff), held.at[g]
            pieces[name].append(links.post(src, dst, peer(k)))

    give("g", 4)
    give("u", 4)
    give("d", 4)

    row = lax.broadcasted_iota(jnp.int32, (32, 128), 0)
    lane = lax.broadcasted_iota(jnp.int32, (32, 128), 1)
    position = row % 4
    for i in range(8):
        position = position + jnp.where(row // 4 == i, lens[z * 8 + i], 0)
    freqs = jnp.exp((lane % 64).astype(F32) * (-2.0 / 128 * math.log(THETA)))
    angles = position.astype(F32) * freqs
    cosine = jnp.cos(angles)
    sine = jnp.where(lane < 64, -jnp.sin(angles), jnp.sin(angles))

    wait_all(flying)
    mean, inverse = moments(stat1, n, 128)
    wait_all(x_fly)

    def block_of(j):
        held = xs[...] if j == 0 else x_all[j - 1]
        return ((held.astype(F32) - mean) * inverse).astype(BF16)

    blocks = [block_of(j) for j in range(4)]

    def project(i):
        loads["w", i].wait()
        wait_all(w_fly[i])
        made = jnp.dot(blocks[0], wqkv_r[i, p], preferred_element_type=F32)
        for j in range(1, 4):
            made = made + jnp.dot(blocks[j], wqkv_r[i, flip(p, j)], preferred_element_type=F32)
        return made.reshape(PLANE, 32, 256)

    def rotate_rows(sums):
        return jnp.concatenate(
            [
                sums[:, i * 128 : (i + 1) * 128] * cosine
                + pltpu.roll(sums[:, i * 128 : (i + 1) * 128], 64, 1) * sine
                for i in range(2)
            ],
            axis=1,
        ).astype(BF16)

    q_part[...] = project(0)
    q_fly = [links.post(q_part.at[flip(z, i)], q_got.at[i - 1], peer(4 * i)) for i in (1, 2, 3)]
    give("g", 5, 6, 3)
    for i in (1, 2):
        kv_part[:, i - 1] = project(i).astype(BF16)
    wait_all(q_fly)
    sums = q_part[z]
    for i in range(3):
        sums = sums + q_got[i]
    q_all[z, p] = rotate_rows(sums)
    q_fly = {k: links.post(q_all.at[z, p], q_all.at[z, p], peer(k)) for k in range(1, n)}
    kv_fly = [
        links.post(kv_part.at[flip(z, i)], kv_got.at[i - 1], peer(4 * i)) for i in (1, 2, 3)
    ]
    give("g", 1, 2, 7)

    loads["k"].wait()
    loads["v"].wait()
    lane16 = lax.broadcasted_iota(jnp.int32, (16, 128), 1)
    row128 = lax.broadcasted_iota(jnp.int32, (128, 128), 0)
    lane128 = lax.broadcasted_iota(jnp.int32, (128, 128), 1)
    same = row128 % 16 // 4 == lane128 // 32
    slot = me * slots + lane128 % 32
    acc_fly, st_fly = {}, {}
    for i in range(4):
        zb = flip(z, i)
        for j in range(4):
            if 4 * i + j:
                q_fly[4 * i + j].wait()
        packs = []
        for half in range(2):
            first = zb * 8 + half * 4
            length = jnp.where(lane128 // 32 == 0, lens[first], 0)
            for a in range(1, 4):
                length = jnp.where(lane128 // 32 == a, lens[first + a], length)
            live = same & (slot < length)
            rows = slice(half * 16, half * 16 + 16)
            scores = jnp.concatenate(
                [
                    lax.dot_general(
                        q_all[zb, h // 2, rows, h % 2 * 128 : h % 2 * 128 + 128],
                        ck[pl.ds(first, 4), :, h * 128 : (h + 1) * 128].reshape(128, 128),
                        (((1,), (1,)), ((), ())),
                        preferred_element_type=F32,
                    )
                    for h in range(8)
                ],
                axis=0,
            )
            scores = jnp.where(live, scores * scale, NEGATIVE)
            top = jnp.max(scores, axis=-1, keepdims=True)
            weights = jnp.where(live, jnp.exp(scores - top), 0.0)
            total = jnp.sum(weights, axis=-1, keepdims=True)
            coarse = weights.astype(BF16)
            fine = (weights - coarse.astype(F32)).astype(BF16)
            pack = jnp.zeros((16, 128), F32)
            for h in range(8):
                mine = slice(h * 16, (h + 1) * 16)
                both = jnp.dot(
                    jnp.concatenate([coarse[mine], fine[mine]], axis=0),
                    cv[pl.ds(first, 4), :, h * 128 : (h + 1) * 128].reshape(128, 128),
                    preferred_element_type=F32,
                )
                acc_part[i, h // 2, rows, h % 2 * 128 : h % 2 * 128 + 128] = (
                    both[0:16] + both[16:32]
                ).astype(BF16)
                at = 8 * (h // 2) + h % 2
                pack = jnp.where(
                    lane16 == at, top[mine], jnp.where(lane16 == at + 2, total[mine], pack)
                )
            packs.append(pack)
        turned = to_lanes(jnp.concatenate(packs, axis=0))
        for q in range(4):
            st_part[i, q] = turned[8 * q : 8 * q + 8]
        for j in range(4):
            k = 4 * i + j
            if k:
                st_fly[k] = links.post(st_part.at[i, flip(p, j)], st_got.at[k - 1], peer(k))
                acc_fly[k] = links.post(acc_part.at[i, flip(p, j)], acc_got.at[k - 1], peer(k))
    give("u", 5, 6, 3)

    wait_all(kv_fly)
    sums_k, sums_v = kv_part[z, 0].astype(F32), kv_part[z, 1].astype(F32)
    for i in range(3):
        sums_k = sums_k + kv_got[i, 0].astype(F32)
        sums_v = sums_v + kv_got[i, 1].astype(F32)
    kv_all[z, p, 0] = rotate_rows(sums_k)
    kv_all[z, p, 1] = sums_v.astype(BF16)
    kv_fly = [links.post(kv_all.at[z, p], kv_all.at[z, p], peer(4 * i)) for i in (1, 2, 3)]
    token = lax.broadcasted_iota(jnp.int32, (32, 32), 0)
    key = lax.broadcasted_iota(jnp.int32, (32, 32), 1)
    allowed = (token // 4 == key // 4) & (key <= token)
    fresh = []
    for j in range(2):
        part = slice(j * 128, (j + 1) * 128)
        scores = (
            lax.dot_general(
                q_all[z, p, :, part],
                kv_all[z, p, 0, :, part],
                (((1,), (1,)), ((), ())),
                preferred_element_type=F32,
            )
            * scale
        )
        fresh.append(jnp.where(allowed, scores, NEGATIVE))

    for k in range(1, n):
        st_fly[k].wait()
    tiles = [st_part[0, p]] + [st_got[k - 1] for k in range(1, n)]
    top = tiles[0]
    for tile in tiles[1:]:
        top = jnp.maximum(top, tile)
    factors = [jnp.exp(tile - top) for tile in tiles]
    total = pltpu.roll(tiles[0], 6, 0) * factors[0]
    for tile, factor in zip(tiles[1:], factors[1:]):
        total = total + pltpu.roll(tile, 6, 0) * factor
    sub = lax.broadcasted_iota(jnp.int32, (8, 128), 0)
    factors[0] = jnp.where(
        sub < 2,
        factors[0],
        jnp.where(sub < 4, pltpu.roll(top, 2, 0), pltpu.roll(total, 4, 0)),
    )
    back = jnp.concatenate(factors, axis=0).T[0:32]
    for k in range(1, n):
        acc_fly[k].wait()
    for j in range(2):
        part = slice(j * 128, (j + 1) * 128)
        summed = acc_part[0, p, :, part].astype(F32) * back[:, j : j + 1]
        for k in range(1, n):
            summed = summed + acc_got[k - 1, :, part].astype(F32) * back[:, 8 * k + j : 8 * k + j + 1]
        top_cache, total_cache = back[:, 2 + j : 3 + j], back[:, 4 + j : 5 + j]
        scores = fresh[j]
        top_all = jnp.maximum(top_cache, jnp.max(scores, axis=-1, keepdims=True))
        weights = jnp.where(allowed, jnp.exp(scores - top_all), 0.0)
        kept = jnp.exp(top_cache - top_all)
        running = total_cache * kept + jnp.sum(weights, axis=-1, keepdims=True)
        summed = summed * kept + jnp.dot(
            weights,
            kv_all[z, p, 1, :, part].astype(F32),
            precision=lax.Precision.HIGHEST,
            preferred_element_type=F32,
        )
        att_all[z, p, :, part] = (summed / running).astype(BF16)
    att_fly = {k: links.post(att_all.at[z, p], att_all.at[z, p], peer(k)) for k in range(1, n)}
    give("u", 1, 2, 7)

    loads["o"].wait()
    for i in range(4):
        zb = flip(z, i)
        for j in range(4):
            if 4 * i + j:
                att_fly[4 * i + j].wait()
        attended = jnp.concatenate([att_all[zb, q] for q in range(4)], axis=1)
        o_mine[zb] = jnp.dot(attended, wo[...], preferred_element_type=F32)
    swap = links.post(o_mine.at[pl.ds(2 * (1 - core), 2)], o_other, partner)
    give("d", 5)
    swap.wait()
    mixed = xs[pl.ds(pl.multiple_of(core * 64, 64), 64)].astype(F32) + (
        o_mine[pl.ds(2 * core, 2)] + o_other[...]
    ).reshape(64, 128)
    mixed_all[g] = mixed
    stat2[me] = pack_sums(mixed)
    flying = [links.post(stat2.at[me], stat2.at[me], peer(k)) for k in range(1, n)]
    mix_fly = [links.post(mixed_all.at[g], mixed_all.at[g], peer(k)) for k in range(1, 8)]
    give("d", 6)
    wait_all(flying)
    mean, inverse = moments(stat2, n, 64)
    wait_all(mix_fly)
    for i in range(8):
        normed2[core, :, i * 128 : (i + 1) * 128] = (
            (mixed_all[i] - mean) * inverse
        ).astype(BF16)
    swap = links.post(normed2.at[core], normed2.at[core], partner)
    loads["g"].wait()
    loads["u"].wait()
    wait_all(pieces["g"])
    swap.wait()
    rows = normed2[...].reshape(128, 1024)
    chunks = gu_mine.shape[0]
    tile = ff // chunks
    gu_fly = []
    for c in range(chunks):
        here = slice(c * tile, (c + 1) * tile)
        gate = jnp.dot(rows, wg_r[:, :, here].reshape(1024, tile), preferred_element_type=F32)
        if c == 0:
            wait_all(pieces["u"])
        up = jnp.dot(rows, wu_r[:, :, here].reshape(1024, tile), preferred_element_type=F32)
        gu_mine[c, 0] = gate
        gu_mine[c, 1] = up
        gu_send[c, 0] = gate.astype(BF16)
        gu_send[c, 1] = up.astype(BF16)
        gu_fly.append(links.post(gu_send.at[c], gu_got.at[c], peer(8)))
        for k in ((7,), (3,), (1,), (2,))[c]:
            give("d", k)
    wait_all(kv_fly)
    kv_fly = [
        links.post(kv_all.at[:, p], kv_all.at[:, p], peer(j)) for j in (1, 2, 3)
    ]
    loads["d"].wait()
    for c in range(chunks):
        here = slice(c * tile, (c + 1) * tile)
        gu_fly[c].wait()
        gate = gu_mine[c, 0] + gu_got[c, 0].astype(F32)
        up = gu_mine[c, 1] + gu_got[c, 1].astype(F32)
        act = (gate / (1.0 + jnp.exp(-gate)) * up).astype(BF16)
        if c == 0:
            wait_all(pieces["d"])
        for i in range(8):
            made = jnp.dot(act, wd_r[i, here], preferred_element_type=F32).reshape(2, 64, 128)
            d_mine[:, i] = made if c == 0 else d_mine[:, i] + made
    swap = links.post(d_mine.at[1 - core], d_other, partner)
    swap.wait()
    sums = d_mine[core] + d_other[...]
    d_send[...] = sums.astype(BF16)
    d_mine[core] = sums
    flying = [links.post(d_send.at[flip(g, k)], d_got.at[k - 1], peer(k)) for k in range(1, 8)]
    wait_all(flying)
    total = d_mine[core, g]
    for k in range(7):
        total = total + d_got[k].astype(F32)
    out_ref[core] = (mixed_all[g] + total).astype(BF16)
    swap = links.post(out_ref.at[core], out_ref.at[core], partner)
    swap.wait()
    wait_all(kv_fly)


def write_kernel(lens, hidden, kv_ref, k_ref, v_ref, out_ref, ko_ref, vo_ref):
    step = pl.program_id(0)
    group, slots, width = k_ref.shape
    base = lax.axis_index("seq") * slots

    @pl.when(step == 0)
    def _():
        out_ref[...] = hidden[...].reshape(out_ref.shape)

    ko_ref[...] = k_ref[...]
    vo_ref[...] = v_ref[...]
    for i in range(group):
        first = lens[step * group + i] - base

        @pl.when((first < slots) & (first > -4))
        def _():
            place = lax.broadcasted_iota(jnp.int32, (slots, 256), 0)
            for c, old, out in ((0, k_ref, ko_ref), (1, v_ref, vo_ref)):
                for q in range(4):
                    part = slice(q * 256, (q + 1) * 256)
                    fresh = kv_ref[step * 2 + i // 8, q, c].astype(F32)[4 * (i % 8) : 4 * (i % 8) + 4]
                    held = old[i, :, part].astype(F32)
                    for t in range(4):
                        held = jnp.where(place == first + t, fresh[t : t + 1], held)
                    out[i, :, part] = held.astype(BF16)


def body_kernels(
    n,
    hidden_in,
    cache_keys,
    cache_values,
    lengths,
    query_weight,
    key_weight,
    value_weight,
    out_weight,
    gate_weight,
    up_weight,
    down_weight,
):
    requests, token_count, narrow = hidden_in.shape
    rows = requests * token_count
    slot_count, local_width = cache_keys.shape[1:]
    score_scale = 1.0 / math.sqrt(D // HEADS)
    ff = gate_weight.shape[1] // 8
    chunks = 4
    struct = jax.ShapeDtypeStruct
    vmem = pl.BlockSpec(memory_space=pltpu.VMEM)
    smem = pl.BlockSpec(memory_space=pltpu.SMEM)
    far = pl.BlockSpec(memory_space=pltpu.HBM)
    hidden_out, kv_all = pl.pallas_call(
        functools.partial(layer_kernel, n, score_scale),
        out_shape=[
            struct((2, rows // 2, narrow), BF16),
            struct((4, PLANE, 2, 32, 256), BF16),
        ],
        in_specs=[smem] + [far] * 10,
        out_specs=[vmem, vmem],
        scratch_shapes=[
            pltpu.VMEM((rows, narrow), BF16),
            pltpu.VMEM((requests, slot_count, local_width), BF16),
            pltpu.VMEM((requests, slot_count, local_width), BF16),
            pltpu.VMEM((local_width, narrow), BF16),
            pltpu.VMEM((3, PLANE, narrow, 256), BF16),
            pltpu.VMEM((8, narrow, ff), BF16),
            pltpu.VMEM((8, narrow, ff), BF16),
            pltpu.VMEM((8, ff, narrow), BF16),
            pltpu.VMEM((n, 8, 128), F32),
            pltpu.VMEM((3, rows, narrow), BF16),
            pltpu.VMEM((4, 32, 256), F32),
            pltpu.VMEM((3, 32, 256), F32),
            pltpu.VMEM((4, 2, 32, 256), BF16),
            pltpu.VMEM((3, 2, 32, 256), BF16),
            pltpu.VMEM((4, PLANE, 32, 256), BF16),
            pltpu.VMEM((4, PLANE, 32, 256), BF16),
            pltpu.VMEM((n - 1, 32, 256), BF16),
            pltpu.VMEM((4, PLANE, 8, 128), F32),
            pltpu.VMEM((n - 1, 8, 128), F32),
            pltpu.VMEM((4, PLANE, 32, 256), BF16),
            pltpu.VMEM((4, 32, narrow), F32),
            pltpu.VMEM((2, 32, narrow), F32),
            pltpu.VMEM((8, rows // 2, narrow), F32),
            pltpu.VMEM((n, 8, 128), F32),
            pltpu.VMEM((2, rows // 2, 8 * narrow), BF16),
            pltpu.VMEM((chunks, 2, rows, ff // chunks), F32),
            pltpu.VMEM((chunks, 2, rows, ff // chunks), BF16),
            pltpu.VMEM((chunks, 2, rows, ff // chunks), BF16),
            pltpu.VMEM((2, 8, rows // 2, narrow), F32),
            pltpu.VMEM((8, rows // 2, narrow), F32),
            pltpu.VMEM((8, rows // 2, narrow), BF16),
            pltpu.VMEM((7, rows // 2, narrow), BF16),
            pltpu.SemaphoreType.DMA((SEMS,)),
            pltpu.SemaphoreType.DMA((SEMS,)),
            pltpu.SemaphoreType.DMA((10,)),
        ],
        compiler_params=pltpu.CompilerParams(
            collective_id=1, has_side_effects=True, vmem_limit_bytes=60 * 2**20
        ),
    )(
        lengths,
        hidden_in.reshape(rows, narrow),
        query_weight,
        key_weight,
        value_weight,
        cache_keys,
        cache_values,
        out_weight,
        gate_weight,
        up_weight,
        down_weight,
    )
    group = 16
    block = pl.BlockSpec((group, slot_count, local_width), lambda s: (s, 0, 0))
    return pl.pallas_call(
        write_kernel,
        grid=(requests // group,),
        out_shape=[
            struct(hidden_in.shape, BF16),
            struct(cache_keys.shape, BF16),
            struct(cache_values.shape, BF16),
        ],
        in_specs=[smem, vmem, vmem, block, block],
        out_specs=[pl.BlockSpec(hidden_in.shape, lambda s: (0, 0, 0)), block, block],
    )(lengths, hidden_out, kv_all, cache_keys, cache_values)


def body(n, model_shards, hidden_in, cache_keys, *rest):
    rows = hidden_in.shape[0] * hidden_in.shape[1]
    tiled = (
        n == 16
        and rows == 128
        and hidden_in.shape[1] == 4
        and hidden_in.shape[2] == 128
        and cache_keys.shape[1] == 32
        and cache_keys.shape[2] == 1024
        and model_shards == 2
    )
    if tiled:
        return body_kernels(n, hidden_in, cache_keys, *rest)
    return body_plain(hidden_in, cache_keys, *rest)


def solution(mesh):
    placed = (
        P(None, None, "seq"),
        P(None, "seq", "mdl"),
        P(None, "seq", "mdl"),
        P(),
        P("seq", "mdl"),
        P("seq", "mdl"),
        P("seq", "mdl"),
        P("mdl", "seq"),
        P("seq", "mdl"),
        P("seq", "mdl"),
        P("mdl", "seq"),
    )
    return jax.shard_map(
        functools.partial(body, mesh.shape["seq"], mesh.shape["mdl"]),
        mesh=mesh,
        in_specs=placed,
        out_specs=(P(None, None, "seq"), P(None, "seq", "mdl"), P(None, "seq", "mdl")),
        check_vma=False,
    )
```

```python
import functools
import math

import jax
import jax.numpy as jnp
from jax import lax
from jax.experimental import pallas as pl
from jax.experimental.pallas import tpu as pltpu
from jax.sharding import PartitionSpec as P

D = 2048
HEADS = 16


EPS = 1e-05
THETA = 10000.0
NEGATIVE = -1e30


def rotate(vectors, placed_pos):
    head_size = vectors.shape[-1]
    half_dim = head_size // 2
    freqs = THETA ** (-jnp.arange(half_dim, dtype=jnp.float32) * 2.0 / head_size)
    angles = placed_pos.astype(jnp.float32)[..., None, None] * freqs
    cosine = jnp.cos(angles)
    sine = jnp.sin(angles)
    first_half = vectors[..., :half_dim]
    second_half = vectors[..., half_dim:]
    return jnp.concatenate(
        [first_half * cosine - second_half * sine, second_half * cosine + first_half * sine],
        axis=-1,
    )


def normalize(widened, row_sums, square_sums):
    row_mean = row_sums / D
    second_moment = square_sums / D
    inverse = 1.0 / jnp.sqrt(second_moment - row_mean * row_mean + EPS)
    return ((widened - row_mean[..., None]) * inverse[..., None]).astype(jnp.bfloat16)


def body_plain(
    hidden_in,
    cache_keys,
    cache_values,
    lengths,
    query_weight,
    key_weight,
    value_weight,
    out_weight,
    gate_weight,
    up_weight,
    down_weight,
):
    requests, token_count, narrow_width = hidden_in.shape
    slot_count = cache_keys.shape[1]
    local_width = cache_keys.shape[2]
    head_size = D // HEADS
    local_heads = local_width // head_size
    score_scale = 1.0 / math.sqrt(head_size)
    shard_index = lax.axis_index("seq")
    slot_ids = shard_index * slot_count + jnp.arange(slot_count, dtype=jnp.int32)
    live_slots = slot_ids[None, :] < lengths[:, None]
    old_keys = cache_keys.reshape(requests, slot_count, local_heads, head_size)
    old_values = cache_values.reshape(requests, slot_count, local_heads, head_size).astype(
        jnp.float32
    )
    positions = lengths[:, None] + jnp.arange(token_count, dtype=jnp.int32)[None, :]
    out_list = []
    key_list = []
    value_list = []
    for token_step in range(1):
        row_block = hidden_in
        block_rows = row_block.shape[1]
        widened = row_block.astype(jnp.float32)
        row_sums, square_sums = lax.psum(
            (jnp.sum(widened, axis=-1), jnp.sum(widened * widened, axis=-1)), "seq"
        )
        normed = normalize(widened, row_sums, square_sums)
        query_part = jnp.einsum(
            "rnc,cm->rnm", normed, query_weight, preferred_element_type=jnp.float32
        )
        key_part = jnp.einsum("rnc,cm->rnm", normed, key_weight, preferred_element_type=jnp.float32)
        value_part = jnp.einsum(
            "rnc,cm->rnm", normed, value_weight, preferred_element_type=jnp.float32
        )
        queries, keys_full, values_full = lax.psum((query_part, key_part, value_part), "seq")
        placed_pos = positions[:, token_step : token_step + block_rows]
        queries = rotate(
            queries.reshape(requests, block_rows, local_heads, head_size), placed_pos
        ).astype(jnp.bfloat16)
        new_key = rotate(
            keys_full.reshape(requests, block_rows, local_heads, head_size), placed_pos
        ).astype(jnp.bfloat16)
        new_value = values_full.reshape(requests, block_rows, local_heads, head_size).astype(
            jnp.bfloat16
        )
        keys_new = jnp.concatenate(key_list + [new_key], axis=1)
        values_new = jnp.concatenate(value_list + [new_value], axis=1)
        old_scores = (
            jnp.einsum("rnhd,rjhd->rnhj", queries, old_keys, preferred_element_type=jnp.float32)
            * score_scale
        )
        old_scores = jnp.where(live_slots[:, None, None, :], old_scores, NEGATIVE)
        top_old = jnp.max(old_scores, axis=-1)
        weights_old = jnp.where(
            live_slots[:, None, None, :], jnp.exp(old_scores - top_old[..., None]), 0.0
        )
        total_old = jnp.sum(weights_old, axis=-1)
        summed_old = jnp.einsum(
            "rnhj,rjhd->rnhd", weights_old, old_values, precision=lax.Precision.HIGHEST
        )
        top_cache = lax.pmax(top_old, "seq")
        factor_old = jnp.exp(top_old - top_cache)
        total_cache, summed_cache = lax.psum(
            (total_old * factor_old, summed_old * factor_old[..., None]), "seq"
        )
        new_scores = (
            jnp.einsum("rnhd,rshd->rnhs", queries, keys_new, preferred_element_type=jnp.float32)
            * score_scale
        )
        key_index = jnp.arange(keys_new.shape[1], dtype=jnp.int32)
        query_index = token_step + jnp.arange(block_rows, dtype=jnp.int32)
        allowed = key_index[None, :] <= query_index[:, None]
        new_scores = jnp.where(allowed[None, :, None, :], new_scores, NEGATIVE)
        top_new = jnp.max(new_scores, axis=-1)
        weights_new = jnp.exp(new_scores - top_new[..., None])
        total_new = jnp.sum(weights_new, axis=-1)
        summed_new = jnp.einsum(
            "rnhs,rshd->rnhd",
            weights_new,
            values_new.astype(jnp.float32),
            precision=lax.Precision.HIGHEST,
        )
        top_score = jnp.maximum(top_cache, top_new)
        factor_cache = jnp.exp(top_cache - top_score)
        factor_new = jnp.exp(top_new - top_score)
        running = total_cache * factor_cache + total_new * factor_new
        combined = summed_cache * factor_cache[..., None] + summed_new * factor_new[..., None]
        attended = (
            (combined / running[..., None])
            .astype(jnp.bfloat16)
            .reshape(requests, block_rows, local_width)
        )
        attn_part = jnp.einsum(
            "rnm,mc->rnc", attended, out_weight, preferred_element_type=jnp.float32
        )
        mixed = widened + lax.psum(attn_part, "mdl")
        sums_mixed, squares_mixed = lax.psum(
            (jnp.sum(mixed, axis=-1), jnp.sum(mixed * mixed, axis=-1)), "seq"
        )
        normed2 = normalize(mixed, sums_mixed, squares_mixed)
        gate_part = jnp.einsum(
            "rnc,cf->rnf", normed2, gate_weight, preferred_element_type=jnp.float32
        )
        up_part = jnp.einsum("rnc,cf->rnf", normed2, up_weight, preferred_element_type=jnp.float32)
        gate_full, up_full = lax.psum((gate_part, up_part), "seq")
        act_full = (jax.nn.silu(gate_full) * up_full).astype(jnp.bfloat16)
        down_part = jnp.einsum(
            "rnf,fc->rnc", act_full, down_weight, preferred_element_type=jnp.float32
        )
        block_out = (mixed + lax.psum(down_part, "mdl")).astype(jnp.bfloat16)
        block_out, new_key, new_value = (block_out, new_key, new_value)
        out_list.append(block_out)
        key_list.append(new_key)
        value_list.append(new_value)
    hidden_out = jnp.concatenate(out_list, axis=1)
    keys_all = jnp.concatenate(key_list, axis=1)
    values_all = jnp.concatenate(value_list, axis=1)
    slot_hits = slot_ids[None, None, :] == positions[:, :, None]
    one_hot = slot_hits.astype(jnp.bfloat16)
    written = jnp.any(slot_hits, axis=1)[..., None]
    placed_keys = jnp.einsum(
        "rts,rtm->rsm",
        one_hot,
        keys_all.reshape(requests, token_count, local_width),
        preferred_element_type=jnp.float32,
    ).astype(jnp.bfloat16)
    placed_values = jnp.einsum(
        "rts,rtm->rsm",
        one_hot,
        values_all.reshape(requests, token_count, local_width),
        preferred_element_type=jnp.float32,
    ).astype(jnp.bfloat16)
    new_cache_keys = jnp.where(written, placed_keys, cache_keys)
    new_cache_values = jnp.where(written, placed_values, cache_values)
    return (hidden_out, new_cache_keys, new_cache_values)


PLANE = 4
MESH = pl.DeviceIdType.MESH
F32 = jnp.float32
BF16 = jnp.bfloat16
SEMS = 208


def flip(value, mask):
    out = value
    for b in range(4):
        if mask >> b & 1:
            out = out + (1 - 2 * (value // (1 << b) % 2)) * (1 << b)
    return out


class Links:
    def __init__(self, send, recv):
        self.send, self.recv, self.used, self.all = send, recv, 0, []

    def post(self, src, dst, device):
        i = self.used
        self.used += 1
        copy = pltpu.make_async_remote_copy(
            src_ref=src,
            dst_ref=dst,
            send_sem=self.send.at[i],
            recv_sem=self.recv.at[i],
            device_id=device,
            device_id_type=MESH,
        )
        copy.start()
        self.all.append(copy)
        return copy


def wait_all(copies):
    for copy in copies:
        copy.wait()


def to_lanes(columns):
    rows = columns.shape[0]
    if rows < 128:
        columns = jnp.concatenate([columns, jnp.zeros((128 - rows, 128), F32)], axis=0)
    return columns.T


def pack_sums(widened):
    rows = widened.shape[0]
    lanes = lax.broadcasted_iota(jnp.int32, (rows, 128), 1)
    first = jnp.sum(widened, axis=-1, keepdims=True)
    second = jnp.sum(widened * widened, axis=-1, keepdims=True)
    return to_lanes(jnp.where(lanes == 0, first, jnp.where(lanes == 1, second, 0.0)))[0:8]


def moments(slots, n, rows):
    total = slots[0]
    for i in range(1, n):
        total = total + slots[i]
    back = jnp.concatenate([total, jnp.zeros((120, 128), F32)], axis=0).T[0:rows]
    mean = back[:, 0:1] / D
    inverse = 1.0 / jnp.sqrt(back[:, 1:2] / D - mean * mean + EPS)
    return mean, inverse


def layer_kernel(
    n,
    scale,
    lens,
    x_hbm,
    wq,
    wk,
    wv,
    ck_hbm,
    cv_hbm,
    wo_hbm,
    wg,
    wu,
    wd,
    out_ref,
    kv_all,
    xs,
    ck,
    cv,
    wo,
    wqkv_r,
    wg_r,
    wu_r,
    wd_r,
    stat1,
    x_all,
    q_part,
    q_got,
    kv_part,
    kv_got,
    q_all,
    acc_part,
    acc_got,
    st_part,
    st_got,
    att_all,
    o_mine,
    o_other,
    mixed_all,
    stat2,
    normed2,
    gu_mine,
    gu_send,
    gu_got,
    d_mine,
    d_other,
    d_send,
    d_got,
    send,
    recv,
    local,
):
    me = lax.axis_index("seq")
    core = lax.axis_index("mdl")
    z, p = me // PLANE, me % PLANE
    g = me % 8
    links = Links(send, recv)
    partner = {"mdl": 1 - core}
    slots = ck.shape[1]
    ff = wg_r.shape[2]
    loads = {}

    def load(name, src, dst):
        copy = pltpu.make_async_copy(src, dst, local.at[len(loads)])
        copy.start()
        loads[name] = copy

    def peer(k):
        return {"seq": flip(me, k)}

    load("x", x_hbm, xs)
    barrier = pltpu.get_barrier_semaphore()
    for k in range(1, n):
        pl.semaphore_signal(barrier, inc=1, device_id=peer(k), device_id_type=MESH)
    pl.semaphore_signal(barrier, inc=1, device_id=partner, device_id_type=MESH)

    def cols(ref, index, width):
        return ref.at[:, pl.ds(pl.multiple_of(index * width, width), width)]

    def rows_of(ref, index, height):
        return ref.at[pl.ds(pl.multiple_of(index * height, height), height)]

    for i, w in enumerate((wq, wk, wv)):
        load(("w", i), cols(w, p, 256), wqkv_r.at[i, p])
    load("k", ck_hbm, ck)
    load("v", cv_hbm, cv)
    load("o", wo_hbm, wo)
    load("g", cols(wg, g, ff), wg_r.at[g])
    load("u", cols(wu, g, ff), wu_r.at[g])
    load("d", rows_of(wd, g, ff), wd_r.at[g])

    loads["x"].wait()
    widened = xs[...].astype(F32)
    stat1[me] = pack_sums(widened)
    pl.semaphore_wait(barrier, n)

    flying = [links.post(stat1.at[me], stat1.at[me], peer(k)) for k in range(1, n)]
    x_fly = [links.post(xs, x_all.at[j - 1], peer(j)) for j in (1, 2, 3)]
    w_fly = [
        [
            links.post(cols(w, flip(p, j), 256), wqkv_r.at[i, p], peer(j))
            for j in (1, 2, 3)
        ]
        for i, w in enumerate((wq, wk, wv))
    ]

    pieces = {"g": [], "u": [], "d": []}

    def give(name, *masks):
        for k in masks:
            if name == "d":
                src, dst = rows_of(wd, flip(g, k), ff), wd_r.at[g]
            else:
                w, held = (wg, wg_r) if name == "g" else (wu, wu_r)
                src, dst = cols(w, flip(g, k), ff), held.at[g]
            pieces[name].append(links.post(src, dst, peer(k)))

    give("g", 4)
    give("u", 4)
    give("d", 4)

    row = lax.broadcasted_iota(jnp.int32, (32, 128), 0)
    lane = lax.broadcasted_iota(jnp.int32, (32, 128), 1)
    position = row % 4
    for i in range(8):
        position = position + jnp.where(row // 4 == i, lens[z * 8 + i], 0)
    freqs = jnp.exp((lane % 64).astype(F32) * (-2.0 / 128 * math.log(THETA)))
    angles = position.astype(F32) * freqs
    cosine = jnp.cos(angles)
    sine = jnp.where(lane < 64, -jnp.sin(angles), jnp.sin(angles))

    wait_all(flying)
    mean, inverse = moments(stat1, n, 128)
    wait_all(x_fly)

    def block_of(j):
        held = xs[...] if j == 0 else x_all[j - 1]
        return ((held.astype(F32) - mean) * inverse).astype(BF16)

    blocks = [block_of(j) for j in range(4)]

    def project(i):
        loads["w", i].wait()
        wait_all(w_fly[i])
        made = jnp.dot(blocks[0], wqkv_r[i, p], preferred_element_type=F32)
        for j in range(1, 4):
            made = made + jnp.dot(blocks[j], wqkv_r[i, flip(p, j)], preferred_element_type=F32)
        return made.reshape(PLANE, 32, 256)

    def rotate_rows(sums):
        return jnp.concatenate(
            [
                sums[:, i * 128 : (i + 1) * 128] * cosine
                + pltpu.roll(sums[:, i * 128 : (i + 1) * 128], 64, 1) * sine
                for i in range(2)
            ],
            axis=1,
        ).astype(BF16)

    q_part[...] = project(0)
    q_fly = [links.post(q_part.at[flip(z, i)], q_got.at[i - 1], peer(4 * i)) for i in (1, 2, 3)]
    give("g", 5, 6, 3)
    for i in (1, 2):
        kv_part[:, i - 1] = project(i).astype(BF16)
    wait_all(q_fly)
    sums = q_part[z]
    for i in range(3):
        sums = sums + q_got[i]
    q_all[z, p] = rotate_rows(sums)
    q_fly = {k: links.post(q_all.at[z, p], q_all.at[z, p], peer(k)) for k in range(1, n)}
    kv_fly = [
        links.post(kv_part.at[flip(z, i)], kv_got.at[i - 1], peer(4 * i)) for i in (1, 2, 3)
    ]
    give("g", 1, 2, 7)

    loads["k"].wait()
    loads["v"].wait()
    lane16 = lax.broadcasted_iota(jnp.int32, (16, 128), 1)
    row128 = lax.broadcasted_iota(jnp.int32, (128, 128), 0)
    lane128 = lax.broadcasted_iota(jnp.int32, (128, 128), 1)
    same = row128 % 16 // 4 == lane128 // 32
    slot = me * slots + lane128 % 32
    acc_fly, st_fly = {}, {}
    for i in range(4):
        zb = flip(z, i)
        for j in range(4):
            if 4 * i + j:
                q_fly[4 * i + j].wait()
        packs = []
        for half in range(2):
            first = zb * 8 + half * 4
            length = jnp.where(lane128 // 32 == 0, lens[first], 0)
            for a in range(1, 4):
                length = jnp.where(lane128 // 32 == a, lens[first + a], length)
            live = same & (slot < length)
            rows = slice(half * 16, half * 16 + 16)
            scores = jnp.concatenate(
                [
                    lax.dot_general(
                        q_all[zb, h // 2, rows, h % 2 * 128 : h % 2 * 128 + 128],
                        ck[pl.ds(first, 4), :, h * 128 : (h + 1) * 128].reshape(128, 128),
                        (((1,), (1,)), ((), ())),
                        preferred_element_type=F32,
                    )
                    for h in range(8)
                ],
                axis=0,
            )
            scores = jnp.where(live, scores * scale, NEGATIVE)
            top = jnp.max(scores, axis=-1, keepdims=True)
            weights = jnp.where(live, jnp.exp(scores - top), 0.0)
            total = jnp.sum(weights, axis=-1, keepdims=True)
            coarse = weights.astype(BF16)
            fine = (weights - coarse.astype(F32)).astype(BF16)
            pack = jnp.zeros((16, 128), F32)
            for h in range(8):
                mine = slice(h * 16, (h + 1) * 16)
                both = jnp.dot(
                    jnp.concatenate([coarse[mine], fine[mine]], axis=0),
                    cv[pl.ds(first, 4), :, h * 128 : (h + 1) * 128].reshape(128, 128),
                    preferred_element_type=F32,
                )
                acc_part[i, h // 2, rows, h % 2 * 128 : h % 2 * 128 + 128] = (
                    both[0:16] + both[16:32]
                ).astype(BF16)
                at = 8 * (h // 2) + h % 2
                pack = jnp.where(
                    lane16 == at, top[mine], jnp.where(lane16 == at + 2, total[mine], pack)
                )
            packs.append(pack)
        turned = to_lanes(jnp.concatenate(packs, axis=0))
        for q in range(4):
            st_part[i, q] = turned[8 * q : 8 * q + 8]
        for j in range(4):
            k = 4 * i + j
            if k:
                st_fly[k] = links.post(st_part.at[i, flip(p, j)], st_got.at[k - 1], peer(k))
                acc_fly[k] = links.post(acc_part.at[i, flip(p, j)], acc_got.at[k - 1], peer(k))
    give("u", 5, 6, 3)

    wait_all(kv_fly)
    sums_k, sums_v = kv_part[z, 0].astype(F32), kv_part[z, 1].astype(F32)
    for i in range(3):
        sums_k = sums_k + kv_got[i, 0].astype(F32)
        sums_v = sums_v + kv_got[i, 1].astype(F32)
    kv_all[z, p, 0] = rotate_rows(sums_k)
    kv_all[z, p, 1] = sums_v.astype(BF16)
    kv_fly = [links.post(kv_all.at[z, p], kv_all.at[z, p], peer(4 * i)) for i in (1, 2, 3)]
    token = lax.broadcasted_iota(jnp.int32, (32, 32), 0)
    key = lax.broadcasted_iota(jnp.int32, (32, 32), 1)
    allowed = (token // 4 == key // 4) & (key <= token)
    fresh = []
    for j in range(2):
        part = slice(j * 128, (j + 1) * 128)
        scores = (
            lax.dot_general(
                q_all[z, p, :, part],
                kv_all[z, p, 0, :, part],
                (((1,), (1,)), ((), ())),
                preferred_element_type=F32,
            )
            * scale
        )
        fresh.append(jnp.where(allowed, scores, NEGATIVE))

    for k in range(1, n):
        st_fly[k].wait()
    tiles = [st_part[0, p]] + [st_got[k - 1] for k in range(1, n)]
    top = tiles[0]
    for tile in tiles[1:]:
        top = jnp.maximum(top, tile)
    factors = [jnp.exp(tile - top) for tile in tiles]
    total = pltpu.roll(tiles[0], 6, 0) * factors[0]
    for tile, factor in zip(tiles[1:], factors[1:]):
        total = total + pltpu.roll(tile, 6, 0) * factor
    sub = lax.broadcasted_iota(jnp.int32, (8, 128), 0)
    factors[0] = jnp.where(
        sub < 2,
        factors[0],
        jnp.where(sub < 4, pltpu.roll(top, 2, 0), pltpu.roll(total, 4, 0)),
    )
    back = jnp.concatenate(factors, axis=0).T[0:32]
    for k in range(1, n):
        acc_fly[k].wait()
    for j in range(2):
        part = slice(j * 128, (j + 1) * 128)
        summed = acc_part[0, p, :, part].astype(F32) * back[:, j : j + 1]
        for k in range(1, n):
            summed = summed + acc_got[k - 1, :, part].astype(F32) * back[:, 8 * k + j : 8 * k + j + 1]
        top_cache, total_cache = back[:, 2 + j : 3 + j], back[:, 4 + j : 5 + j]
        scores = fresh[j]
        top_all = jnp.maximum(top_cache, jnp.max(scores, axis=-1, keepdims=True))
        weights = jnp.where(allowed, jnp.exp(scores - top_all), 0.0)
        kept = jnp.exp(top_cache - top_all)
        running = total_cache * kept + jnp.sum(weights, axis=-1, keepdims=True)
        summed = summed * kept + jnp.dot(
            weights,
            kv_all[z, p, 1, :, part].astype(F32),
            precision=lax.Precision.HIGHEST,
            preferred_element_type=F32,
        )
        att_all[z, p, :, part] = (summed / running).astype(BF16)
    att_fly = {k: links.post(att_all.at[z, p], att_all.at[z, p], peer(k)) for k in range(1, n)}
    give("u", 1, 2, 7)

    loads["o"].wait()
    for i in range(4):
        zb = flip(z, i)
        for j in range(4):
            if 4 * i + j:
                att_fly[4 * i + j].wait()
        attended = jnp.concatenate([att_all[zb, q] for q in range(4)], axis=1)
        o_mine[zb] = jnp.dot(attended, wo[...], preferred_element_type=F32)
    swap = links.post(o_mine.at[pl.ds(2 * (1 - core), 2)], o_other, partner)
    give("d", 5)
    swap.wait()
    mixed = xs[pl.ds(pl.multiple_of(core * 64, 64), 64)].astype(F32) + (
        o_mine[pl.ds(2 * core, 2)] + o_other[...]
    ).reshape(64, 128)
    mixed_all[g] = mixed
    stat2[me] = pack_sums(mixed)
    flying = [links.post(stat2.at[me], stat2.at[me], peer(k)) for k in range(1, n)]
    mix_fly = [links.post(mixed_all.at[g], mixed_all.at[g], peer(k)) for k in range(1, 8)]
    give("d", 6)
    wait_all(kv_fly)
    kv_fly = [
        links.post(kv_all.at[:, p], kv_all.at[:, p], peer(j)) for j in (1, 2, 3)
    ]
    wait_all(flying)
    mean, inverse = moments(stat2, n, 64)
    wait_all(mix_fly)
    for i in range(8):
        normed2[core, :, i * 128 : (i + 1) * 128] = (
            (mixed_all[i] - mean) * inverse
        ).astype(BF16)
    swap = links.post(normed2.at[core], normed2.at[core], partner)
    loads["g"].wait()
    loads["u"].wait()
    wait_all(pieces["g"])
    swap.wait()
    rows = normed2[...].reshape(128, 1024)
    chunks = gu_mine.shape[0]
    tile = ff // chunks
    gu_fly = []
    for c in range(chunks):
        here = slice(c * tile, (c + 1) * tile)
        gate = jnp.dot(rows, wg_r[:, :, here].reshape(1024, tile), preferred_element_type=F32)
        if c == 0:
            wait_all(pieces["u"])
        up = jnp.dot(rows, wu_r[:, :, here].reshape(1024, tile), preferred_element_type=F32)
        gu_mine[c, 0] = gate
        gu_mine[c, 1] = up
        gu_send[c, 0] = gate.astype(BF16)
        gu_send[c, 1] = up.astype(BF16)
        gu_fly.append(links.post(gu_send.at[c], gu_got.at[c], peer(8)))
        for k in ((7,), (3,), (1,), (2,))[c]:
            give("d", k)
    loads["d"].wait()
    for c in range(chunks):
        here = slice(c * tile, (c + 1) * tile)
        gu_fly[c].wait()
        gate = gu_mine[c, 0] + gu_got[c, 0].astype(F32)
        up = gu_mine[c, 1] + gu_got[c, 1].astype(F32)
        act = (gate / (1.0 + jnp.exp(-gate)) * up).astype(BF16)
        if c == 0:
            wait_all(pieces["d"])
        for i in range(8):
            made = jnp.dot(act, wd_r[i, here], preferred_element_type=F32).reshape(2, 64, 128)
            d_mine[:, i] = made if c == 0 else d_mine[:, i] + made
    swap = links.post(d_mine.at[1 - core], d_other, partner)
    swap.wait()
    sums = d_mine[core] + d_other[...]
    d_send[...] = sums.astype(BF16)
    d_mine[core] = sums
    flying = [links.post(d_send.at[flip(g, k)], d_got.at[k - 1], peer(k)) for k in range(1, 8)]
    wait_all(flying)
    total = d_mine[core, g]
    for k in range(7):
        total = total + d_got[k].astype(F32)
    out_ref[core] = (mixed_all[g] + total).astype(BF16)
    swap = links.post(out_ref.at[core], out_ref.at[core], partner)
    swap.wait()
    wait_all(kv_fly)


def write_kernel(lens, hidden, kv_ref, k_ref, v_ref, out_ref, ko_ref, vo_ref):
    step = pl.program_id(0)
    group, slots, width = k_ref.shape
    base = lax.axis_index("seq") * slots

    @pl.when(step == 0)
    def _():
        out_ref[...] = hidden[...].reshape(out_ref.shape)

    ko_ref[...] = k_ref[...]
    vo_ref[...] = v_ref[...]
    for i in range(group):
        first = lens[step * group + i] - base

        @pl.when((first < slots) & (first > -4))
        def _():
            place = lax.broadcasted_iota(jnp.int32, (slots, 256), 0)
            for c, old, out in ((0, k_ref, ko_ref), (1, v_ref, vo_ref)):
                for q in range(4):
                    part = slice(q * 256, (q + 1) * 256)
                    fresh = kv_ref[step * 2 + i // 8, q, c].astype(F32)[4 * (i % 8) : 4 * (i % 8) + 4]
                    held = old[i, :, part].astype(F32)
                    for t in range(4):
                        held = jnp.where(place == first + t, fresh[t : t + 1], held)
                    out[i, :, part] = held.astype(BF16)


def body_kernels(
    n,
    hidden_in,
    cache_keys,
    cache_values,
    lengths,
    query_weight,
    key_weight,
    value_weight,
    out_weight,
    gate_weight,
    up_weight,
    down_weight,
):
    requests, token_count, narrow = hidden_in.shape
    rows = requests * token_count
    slot_count, local_width = cache_keys.shape[1:]
    score_scale = 1.0 / math.sqrt(D // HEADS)
    ff = gate_weight.shape[1] // 8
    chunks = 4
    struct = jax.ShapeDtypeStruct
    vmem = pl.BlockSpec(memory_space=pltpu.VMEM)
    smem = pl.BlockSpec(memory_space=pltpu.SMEM)
    far = pl.BlockSpec(memory_space=pltpu.HBM)
    hidden_out, kv_all = pl.pallas_call(
        functools.partial(layer_kernel, n, score_scale),
        out_shape=[
            struct((2, rows // 2, narrow), BF16),
            struct((4, PLANE, 2, 32, 256), BF16),
        ],
        in_specs=[smem] + [far] * 10,
        out_specs=[vmem, vmem],
        scratch_shapes=[
            pltpu.VMEM((rows, narrow), BF16),
            pltpu.VMEM((requests, slot_count, local_width), BF16),
            pltpu.VMEM((requests, slot_count, local_width), BF16),
            pltpu.VMEM((local_width, narrow), BF16),
            pltpu.VMEM((3, PLANE, narrow, 256), BF16),
            pltpu.VMEM((8, narrow, ff), BF16),
            pltpu.VMEM((8, narrow, ff), BF16),
            pltpu.VMEM((8, ff, narrow), BF16),
            pltpu.VMEM((n, 8, 128), F32),
            pltpu.VMEM((3, rows, narrow), BF16),
            pltpu.VMEM((4, 32, 256), F32),
            pltpu.VMEM((3, 32, 256), F32),
            pltpu.VMEM((4, 2, 32, 256), BF16),
            pltpu.VMEM((3, 2, 32, 256), BF16),
            pltpu.VMEM((4, PLANE, 32, 256), BF16),
            pltpu.VMEM((4, PLANE, 32, 256), BF16),
            pltpu.VMEM((n - 1, 32, 256), BF16),
            pltpu.VMEM((4, PLANE, 8, 128), F32),
            pltpu.VMEM((n - 1, 8, 128), F32),
            pltpu.VMEM((4, PLANE, 32, 256), BF16),
            pltpu.VMEM((4, 32, narrow), F32),
            pltpu.VMEM((2, 32, narrow), F32),
            pltpu.VMEM((8, rows // 2, narrow), F32),
            pltpu.VMEM((n, 8, 128), F32),
            pltpu.VMEM((2, rows // 2, 8 * narrow), BF16),
            pltpu.VMEM((chunks, 2, rows, ff // chunks), F32),
            pltpu.VMEM((chunks, 2, rows, ff // chunks), BF16),
            pltpu.VMEM((chunks, 2, rows, ff // chunks), BF16),
            pltpu.VMEM((2, 8, rows // 2, narrow), F32),
            pltpu.VMEM((8, rows // 2, narrow), F32),
            pltpu.VMEM((8, rows // 2, narrow), BF16),
            pltpu.VMEM((7, rows // 2, narrow), BF16),
            pltpu.SemaphoreType.DMA((SEMS,)),
            pltpu.SemaphoreType.DMA((SEMS,)),
            pltpu.SemaphoreType.DMA((10,)),
        ],
        compiler_params=pltpu.CompilerParams(
            collective_id=1, has_side_effects=True, vmem_limit_bytes=60 * 2**20
        ),
    )(
        lengths,
        hidden_in.reshape(rows, narrow),
        query_weight,
        key_weight,
        value_weight,
        cache_keys,
        cache_values,
        out_weight,
        gate_weight,
        up_weight,
        down_weight,
    )
    group = 16
    block = pl.BlockSpec((group, slot_count, local_width), lambda s: (s, 0, 0))
    return pl.pallas_call(
        write_kernel,
        grid=(requests // group,),
        out_shape=[
            struct(hidden_in.shape, BF16),
            struct(cache_keys.shape, BF16),
            struct(cache_values.shape, BF16),
        ],
        in_specs=[smem, vmem, vmem, block, block],
        out_specs=[pl.BlockSpec(hidden_in.shape, lambda s: (0, 0, 0)), block, block],
    )(lengths, hidden_out, kv_all, cache_keys, cache_values)


def body(n, model_shards, hidden_in, cache_keys, *rest):
    rows = hidden_in.shape[0] * hidden_in.shape[1]
    tiled = (
        n == 16
        and rows == 128
        and hidden_in.shape[1] == 4
        and hidden_in.shape[2] == 128
        and cache_keys.shape[1] == 32
        and cache_keys.shape[2] == 1024
        and model_shards == 2
    )
    if tiled:
        return body_kernels(n, hidden_in, cache_keys, *rest)
    return body_plain(hidden_in, cache_keys, *rest)


def solution(mesh):
    placed = (
        P(None, None, "seq"),
        P(None, "seq", "mdl"),
        P(None, "seq", "mdl"),
        P(),
        P("seq", "mdl"),
        P("seq", "mdl"),
        P("seq", "mdl"),
        P("mdl", "seq"),
        P("seq", "mdl"),
        P("seq", "mdl"),
        P("mdl", "seq"),
    )
    return jax.shard_map(
        functools.partial(body, mesh.shape["seq"], mesh.shape["mdl"]),
        mesh=mesh,
        in_specs=placed,
        out_specs=(P(None, None, "seq"), P(None, "seq", "mdl"), P(None, "seq", "mdl")),
        check_vma=False,
    )
```
